32 devices in a mesh: groups: 2 (over y), row: 4 (over z), col: 4 (over x, core).
Axes of the slice: x: 2, y: 2, z: 4, core: 2. Of those that a mesh axis runs over, the one named last changes fastest.
Arguments:
- slip: float32 [32, 16, 243], P(('groups', 'row', 'col')), parts along dimension 0, may hold values from -6 to 6
- inverse: float32 [32, 486, 243], P(('groups', 'row', 'col')), parts along dimension 0, may hold values from -0.6 to 0.6
- positions: float32 [32, 3, 81], P('groups'), parts along dimension 0
Outputs:
- updated: float32 [32, 16, 243], P(('groups', 'row', 'col')), parts along dimension 0
- residual: float32 [32, 16, 243], P(('groups', 'row', 'col')), parts along dimension 0
The draws below stay inside these ranges and needn't reach their ends.
There are 2 independent parts, one for each index of `groups`. The reference program is written for one: setup_inputs(seed, part) draws one part's arguments, and reference() takes and returns one part's arrays. A program takes and returns all parts, laid end to end along the dimension named above; each array names one. Nothing has to cross between parts.
All inputs are finite; a program needn't handle non-finite values.
Results may differ from the reference program's by a relative error of at most 0.0041.
Values may be sent and summed in bfloat16 or wider, within the bound.
A program may use at most 64 MiB of HBM per device.

```python
import math
import jax
import jax.numpy as jnp
from jax import lax

BLOBS = 162
COLS = 16
HALF = 81
BLOCKS = 16
BODIES = 8


def draw_inverse(key, part):
    matrix_order = 3 * BLOBS
    narrow = 3 * HALF
    spread = 0.35 / math.sqrt(matrix_order)
    diagonal = jax.random.uniform(jax.random.fold_in(key, 12), (BLOCKS, narrow), jnp.float32, 0.2, 0.4)
    off_diag = jax.random.uniform(jax.random.fold_in(key, 11), (BLOCKS, matrix_order, narrow), jnp.float32, -spread, spread)
    row_ids = jnp.arange(matrix_order, dtype=jnp.int32)[None, :, None]
    col_ids = jnp.arange(narrow, dtype=jnp.int32)[None, None, :]
    half_ids = (jnp.arange(BLOCKS, dtype=jnp.int32) % 2)[:, None, None]
    on_diag = row_ids == half_ids * narrow + col_ids
    return off_diag + jnp.where(on_diag, diagonal[:, None, :], 0.0)


def draw_positions(key, part):
    lattice_side = int(math.ceil(BODIES ** (1.0 / 3.0)))
    if lattice_side ** 3 < BODIES:
        lattice_side = lattice_side + 1
    spacing = 8.0
    jitter = 1.0
    step_lo = 1.5
    step_hi = 2.5
    lattice_sites = jax.random.permutation(jax.random.fold_in(key, 21), lattice_side ** 3)[:BODIES]
    grid_coords = jnp.stack([lattice_sites // (lattice_side * lattice_side), lattice_sites // lattice_side % lattice_side, lattice_sites % lattice_side], axis=1).astype(jnp.float32)
    centers = grid_coords * spacing + jax.random.uniform(jax.random.fold_in(key, 22), (BODIES, 3), jnp.float32, -jitter, jitter)
    directions = jax.random.normal(jax.random.fold_in(key, 23), (BODIES, 3, BLOBS), jnp.float32)
    directions = directions / jnp.sqrt(jnp.sum(directions * directions, axis=1, keepdims=True) + 1e-06)
    step_length = jax.random.uniform(jax.random.fold_in(key, 24), (BODIES, 1, BLOBS), jnp.float32, step_lo, step_hi)
    path = jnp.cumsum(directions * step_length, axis=2)
    path = path - jnp.mean(path, axis=2, keepdims=True)
    placed = centers[:, :, None] + path
    return placed.reshape(BODIES, 3, 2, HALF).transpose(0, 2, 1, 3).reshape(BLOCKS, 3, HALF)


def block_scale(rng, dims, shards, low, high):
    def one(axis_at, parts):
        steps = jax.random.uniform(jax.random.fold_in(jax.random.fold_in(rng, 6), axis_at), (parts,), jnp.float32, low / len(shards), high / len(shards))
        return jnp.repeat(jnp.exp(steps), dims[axis_at] // parts).reshape((-1,) + (1,) * (len(dims) - axis_at - 1))

    loudness = one(*shards[0])
    for cut in shards[1:]:
        loudness = loudness * one(*cut)
    return loudness


def centred(rng, shape, scale, most, split=(), kind=jnp.bfloat16):
    factor_of = block_scale(rng, shape, split, -0.22, 0.18) if split else 1.0
    drawn = jax.random.normal(rng, shape, jnp.float32) * scale * factor_of
    return jnp.minimum(jnp.maximum(drawn, -most), most).astype(kind)


def setup_inputs(seed: int = 0, part: int = 0) -> dict:
    key_list = jax.random.split(jax.random.key(seed), 4)
    part_splits = jax.random.split(jax.random.fold_in(key_list[3], part), 4)
    return {
        "slip": centred(part_splits[0], (BLOCKS, COLS, 3 * HALF), 1.0, 6.0, ((0, 16),), jnp.float32),
        "inverse": draw_inverse(jax.random.fold_in(jax.random.fold_in(key_list[3], part), 71), part),
        "positions": draw_positions(jax.random.fold_in(jax.random.fold_in(key_list[3], part), 71), part),
    }


def rpy_tiles(left_pos, right_pos):
    separation = left_pos[:, :, :, None] - right_pos[:, :, None, :]
    dist_sq = lax.optimization_barrier(jnp.sum(separation * separation, axis=1))
    distance = jnp.sqrt(dist_sq)
    far_dist = jnp.maximum(distance, 2.0)
    near_safe = jnp.where(dist_sq > 0.0, distance, 1.0)
    far_mask = dist_sq >= 4.0
    isotropic = jnp.where(far_mask, 0.75 / far_dist * (1.0 + 2.0 / (3.0 * far_dist * far_dist)), 1.0 - 9.0 * distance / 32.0)
    anisotropic = jnp.where(far_mask, 0.75 / far_dist * (1.0 - 2.0 / (far_dist * far_dist)) / (far_dist * far_dist), 3.0 / (32.0 * near_safe))
    first_part = separation[:, :, :, None, :]
    second_part = jnp.swapaxes(separation, 1, 2)[:, None, :, :, :]
    tensor = anisotropic[:, None, :, None, :] * first_part * second_part
    identity_part = jnp.eye(3, dtype=jnp.float32)[None, :, None, :, None]
    tensor = tensor + identity_part * isotropic[:, None, :, None, :]
    tile_count = left_pos.shape[0]
    matrix_order = 3 * left_pos.shape[2]
    return tensor.reshape(tile_count, matrix_order, matrix_order).astype(jnp.bfloat16)

def join_halves(values):
    return values.reshape(BODIES, 2, COLS, 3 * HALF).transpose(0, 2, 1, 3).reshape(BODIES, COLS, 6 * HALF)

def reference(slip, inverse, positions):
    inverse_pairs = inverse.reshape(BODIES, 2, 6 * HALF, 3 * HALF)
    force = jnp.einsum('bsq,bhqp->bhsp', join_halves(slip), inverse_pairs, precision=lax.Precision.HIGHEST).reshape(BLOCKS, COLS, 3 * HALF)
    force_wire = lax.optimization_barrier(force.astype(jnp.bfloat16)).astype(jnp.float32)

    def one_row(row_index):
        left_pos = jnp.broadcast_to(positions[row_index][None], positions.shape)
        tile_blocks = rpy_tiles(left_pos, positions).astype(jnp.float32)
        return jnp.einsum('qsc,qrc->sr', force_wire, tile_blocks, precision=lax.Precision.HIGHEST)
    velocity = lax.map(one_row, jnp.arange(BLOCKS, dtype=jnp.int32))
    residual = slip - velocity
    correction = jnp.einsum('bsq,bhqp->bhsp', join_halves(residual), inverse_pairs, precision=lax.Precision.HIGHEST).reshape(BLOCKS, COLS, 3 * HALF)
    return (force + correction, residual)
```

```python
import functools

import jax
import jax.numpy as jnp
from jax import lax
from jax.experimental import pallas as pl
from jax.experimental.pallas import tpu as pltpu
from jax.sharding import PartitionSpec as P

MESH = pl.DeviceIdType.MESH
LANES = 128
CHUNK = 16
EXTRA = 3


def round_up(value, step):
    return -(-value // step) * step


def split(value):
    high = value.astype(jnp.bfloat16)
    low = (value - high.astype(jnp.float32)).astype(jnp.bfloat16)
    return high, low


def triple(rows, blobs):
    lane = lax.broadcasted_iota(jnp.int32, rows.shape, rows.ndim - 1)
    axis = rows.ndim - 1
    once = pltpu.roll(rows, blobs, axis)
    twice = pltpu.roll(rows, 2 * blobs, axis)
    return jnp.where(lane < blobs, rows, jnp.where(lane < 2 * blobs, once, twice))


def kernel(
    row_count, col_count, blobs, extra,
    slip_hbm, inverse_hbm, positions_hbm,
    updated, residual,
    slip, inverse, positions,
    inv_high, inv_low, tiles, own_rows, own, source, other_slip, part, other_part,
    forces, cross_forces, held, base, far_part, turned, last,
    load_sems, slip_sems, part_sems, send_sems, recv_sems, cross_sems,
    go, ready,
):
    bodies = row_count * col_count // 2
    row = lax.axis_index("row")
    col = lax.axis_index("col")
    half = lax.rem(col, 2)
    partner = col + 1 - 2 * half
    body = (row * col_count + col) // 2
    narrow = 3 * blobs
    wide = source.shape[-1]
    pad = own.shape[2]
    low_side = body < bodies // 2
    lead = body == 0

    def far(step):
        return jnp.where(low_side, bodies - 1 - step, step)

    def same(j):
        there = 2 * j + half
        return {"row": there // col_count, "col": lax.rem(there, col_count)}

    def cross(j):
        there = 2 * j + 1 - half
        return {"row": there // col_count, "col": lax.rem(there, col_count)}

    def loop(start, stop, action):
        def visit(j, carry):
            action(j)
            return carry

        lax.fori_loop(start, stop, visit, 0)

    def signal(sem, device):
        pl.semaphore_signal(sem, inc=1, device_id=device, device_id_type=MESH)

    barrier = pltpu.get_barrier_semaphore()

    @pl.when(half == 0)
    def _():
        signal(barrier, {"col": partner})

    loads = [
        pltpu.make_async_copy(inverse_hbm.at[:, 0, :], inverse, load_sems.at[0]),
        pltpu.make_async_copy(slip_hbm.at[0], slip, load_sems.at[1]),
        pltpu.make_async_copy(positions_hbm, positions, load_sems.at[2]),
    ]
    for load in loads:
        load.start()

    def swap(source_ref, target_ref, sems):
        return pltpu.make_async_remote_copy(
            src_ref=source_ref,
            dst_ref=target_ref,
            send_sem=sems.at[0],
            recv_sem=sems.at[1],
            device_id={"col": partner},
            device_id_type=MESH,
        )

    slip_swap = swap(slip_hbm.at[0], other_slip, slip_sems)

    def first(j):
        there = 2 * j
        return {"row": there // col_count, "col": lax.rem(there, col_count)}

    @pl.when(half == 1)
    def _():
        pl.semaphore_wait(barrier, jnp.where(lead, 1, 3))
        signal(go.at[0], {"col": partner})
        slip_swap.start()

    def greet(j):
        there = 2 * j + jnp.where(lead, 1, 0)
        signal(barrier, {"row": there // col_count, "col": lax.rem(there, col_count)})

    loop(body + 1, bodies, greet)

    @pl.when(half == 0)
    def _():
        pl.semaphore_wait(go.at[0], 1)
        slip_swap.start()

    @pl.when(jnp.logical_not(lead))
    def _():
        signal(ready.at[body], same(0))

        @pl.when((half == 0) & (body > 1))
        def _():
            pl.semaphore_wait(barrier, 2 * (body - 1))

        @pl.when(half == 0)
        def _():
            signal(go.at[1], {"col": partner})

    inv_high[...] = jnp.zeros_like(inv_high)
    inv_low[...] = jnp.zeros_like(inv_low)
    own_rows[...] = jnp.zeros_like(own_rows)

    def build(step, carry):
        j = step // 2
        t = lax.rem(step, 2)
        block = jnp.where(j < bodies, 2 * j + half, 2 * (2 * bodies - 1 - j) + 1 - half)
        lane = lax.broadcasted_iota(jnp.int32, (CHUNK, wide), 1)
        masks = [(lane >= a * blobs) & (lane < (a + 1) * blobs) for a in range(3)]
        there = [
            jnp.broadcast_to(source[a, pl.ds(block, 1), :], (CHUNK, wide)) for a in range(4)
        ]
        for at in range(0, pad, CHUNK):
            d0, d1, d2, db = [own[t, a, at : at + CHUNK, :] - there[a] for a in range(4)]
            dist_sq = d0 * d0 + d1 * d1 + d2 * d2
            r = lax.rsqrt(jnp.where(dist_sq > 0.0, dist_sq, 1.0))
            r2 = r * r
            k = 0.75 * r
            u = k * r2
            apart = dist_sq >= 4.0
            isotropic = jnp.where(
                apart, k + (2.0 / 3.0) * u, 1.0 - (9.0 / 32.0) * (dist_sq * r)
            )
            anisotropic = jnp.where(apart, u - (2.0 * u) * r2, (3.0 / 32.0) * r)
            scaled = anisotropic * db
            for a, da in enumerate((d0, d1, d2)):
                value = scaled * da + jnp.where(masks[a], isotropic, 0.0)
                tiles[j, t, a * pad + at : a * pad + at + CHUNK, :] = value.astype(jnp.bfloat16)
        return carry

    def apply(values, h):
        high, low = split(jnp.pad(values, ((0, 0), (0, wide - narrow))))
        big = inv_high[h]
        small = inv_low[h]
        rows = values.shape[0]
        both = jnp.dot(
            jnp.concatenate([high, low], axis=0), big, preferred_element_type=jnp.float32
        )
        cross = jnp.dot(high, small, preferred_element_type=jnp.float32)
        return both[:rows] + (both[rows:] + cross)

    @pl.when(jnp.logical_not(lead) & (half == 1))
    def _():
        pl.semaphore_wait(go.at[1], 1)

    loop(1, body, lambda j: signal(ready.at[body], same(j)))

    loads[0].wait()
    for h in range(2):
        high, low = split(inverse[h * narrow : (h + 1) * narrow, :])
        inv_high[h, :narrow, :narrow] = high
        inv_low[h, :narrow, :narrow] = low
    loads[1].wait()
    force = apply(slip[...], half)
    slip_swap.wait_recv()
    force = force + apply(other_slip[...], 1 - half)
    forces[body] = force.astype(jnp.bfloat16)
    held[...] = force

    def send(j):
        return pltpu.make_async_remote_copy(
            src_ref=forces.at[body],
            dst_ref=forces.at[body],
            send_sem=send_sems.at[j],
            recv_sem=recv_sems.at[body],
            device_id=same(j),
            device_id_type=MESH,
        )

    slot = bodies - 1 - body
    doubled = (slot < extra) & jnp.logical_not(lead)

    def cross_send():
        return pltpu.make_async_remote_copy(
            src_ref=forces.at[body],
            dst_ref=cross_forces.at[slot],
            send_sem=cross_sems.at[extra],
            recv_sem=cross_sems.at[slot],
            device_id=cross(0),
            device_id_type=MESH,
        )

    @pl.when(jnp.logical_not(lead))
    def _():
        send(0).start()

    @pl.when(doubled)
    def _():
        cross_send().start()

    loop(1, body, lambda j: send(j).start())

    loads[2].wait()
    lane = lax.broadcasted_iota(jnp.int32, source.shape[1:], 1)
    spread = []
    for a in range(3):
        rows = jnp.pad(positions[a], ((0, 0), (0, wide - blobs)))
        spread.append(triple(rows, blobs))
        source[a] = spread[a]
        for t in range(2):
            own_rows[3 * t + a : 3 * t + a + 1, :blobs] = positions[a, pl.ds(2 * body + t, 1), :]
    source[3] = jnp.where(
        lane < blobs, spread[0], jnp.where(lane < 2 * blobs, spread[1], spread[2])
    )
    own_cols = own_rows[...].T
    lane = lax.broadcasted_iota(jnp.int32, (pad, wide), 1)
    for t in range(2):
        cols = [
            jnp.broadcast_to(own_cols[:pad, 3 * t + a : 3 * t + a + 1], (pad, wide))
            for a in range(3)
        ]
        for a in range(3):
            own[t, a] = cols[a]
        own[t, 3] = jnp.where(lane < blobs, cols[0], jnp.where(lane < 2 * blobs, cols[1], cols[2]))

    count = jnp.where(lead, 2 * (bodies + extra), 2 * bodies)
    cut = jnp.where(lead, count, bodies)
    lax.fori_loop(0, cut, build, 0)

    def send_on(j):
        pl.semaphore_wait(ready.at[j], 1)
        send(j).start()

    loop(body + 1, bodies, send_on)
    lax.fori_loop(cut, count, build, 0)

    def product(values, j):
        return lax.dot_general(
            values,
            tiles[j].reshape(6 * pad, wide),
            (((1,), (1,)), ((), ())),
            preferred_element_type=jnp.float32,
        )

    def receive(j):
        pltpu.make_async_remote_copy(
            src_ref=forces.at[j],
            dst_ref=forces.at[j],
            send_sem=send_sems.at[0],
            recv_sem=recv_sems.at[j],
            device_id={"col": partner},
            device_id_type=MESH,
        ).wait_recv()

    def cross_receive(f):
        pltpu.make_async_remote_copy(
            src_ref=cross_forces.at[f],
            dst_ref=cross_forces.at[f],
            send_sem=cross_sems.at[extra],
            recv_sem=cross_sems.at[f],
            device_id={"col": partner},
            device_id_type=MESH,
        ).wait_recv()

    def gather(picks):
        for j in picks:

            @pl.when(j != body)
            def _(j=j):
                receive(j)

        total = product(forces[picks[0]], picks[0])
        for j in picks[1:]:
            total = total + product(forces[j], j)
        return total

    def gather_run(start, stop):
        if stop - start <= 8:
            size = (stop - start + 1) // 2
            total = gather([far(bodies - 1 - k) for k in range(start, start + size)])
            return total + gather([far(bodies - 1 - k) for k in range(start + size, stop)])
        return lax.fori_loop(
            start,
            stop,
            lambda k, total: total + gather([far(bodies - 1 - k)]),
            jnp.zeros((slip.shape[0], 6 * pad), jnp.float32),
        )

    def compact(total):
        full = round_up(6 * pad, LANES)
        total = jnp.pad(total, ((0, 0), (0, full - 6 * pad)))
        lane = lax.broadcasted_iota(jnp.int32, total.shape, 1)

        def moved(by):
            return pltpu.roll(total, full - by, 1) if by else total

        values = []
        for t in range(2):
            start = 3 * t * pad
            shift = pad - blobs
            value = jnp.where(
                lane < blobs,
                moved(start),
                jnp.where(lane < 2 * blobs, moved(start + shift), moved(start + 2 * shift)),
            )
            values.append(value[:, :wide])
        return values

    part_swap = swap(part, other_part, part_sems)

    def share(total):
        for t, value in enumerate(compact(total)):
            part[t] = value
        part_swap.start()

    def settle(more):
        part_swap.wait()
        sums = [part[t] + other_part[t] for t in (half, 1 - half)]
        if more:
            sums = [value + far_part[t] for value, t in zip(sums, (half, 1 - half))]
        mine = slip[...] - sums[0][:, :narrow]
        theirs = other_slip[...] - sums[1][:, :narrow]
        return mine, held[...] + (apply(mine, half) + apply(theirs, 1 - half))

    @pl.when(jnp.logical_not(lead))
    def _():
        share(gather_run(0, bodies))
        mine, result = settle(False)
        residual[0] = mine
        updated[0] = result[:, :narrow]

    @pl.when(lead)
    def _():
        row_at = lax.broadcasted_iota(jnp.int32, (wide, 3 * pad), 0)
        col_at = lax.broadcasted_iota(jnp.int32, (wide, 3 * pad), 1)
        gap = pad - blobs
        wanted = row_at + jnp.where(row_at < blobs, 0, jnp.where(row_at < 2 * blobs, gap, 2 * gap))
        picked = jnp.where((col_at == wanted) & (row_at < narrow), 1.0, 0.0).astype(jnp.bfloat16)
        for s, block in enumerate((bodies - 1, bodies)):
            lanes = slice(s * wide, (s + 1) * wide)
            folded = jnp.zeros((wide, wide), jnp.float32)
            for t in range(2):
                tight = jnp.dot(picked, tiles[block, t], preferred_element_type=jnp.float32)
                tight = tight.astype(jnp.bfloat16)
                turned[t] = tight
                for side in (inv_high, inv_low):
                    folded = folded + lax.dot_general(
                        side[t], tight, (((0,), (0,)), ((), ())), preferred_element_type=jnp.float32
                    )
            high, low = split(folded)
            last[:wide, lanes] = turned[half]
            last[wide : 2 * wide, lanes] = high
            last[2 * wide :, lanes] = low

        share(gather_run(0, bodies - extra))

        if extra > 1:
            for f in range(1, extra):
                receive(bodies - 1 - f)
                cross_receive(f)
            total = jnp.zeros((slip.shape[0], 6 * pad), jnp.float32)
            for f in range(1, extra):
                total = total + product(forces[bodies - 1 - f], bodies - 1 - f)
                total = total + product(cross_forces[f], bodies + f)
            for t, value in enumerate(compact(total)):
                far_part[t] = value

        mine, result = settle(extra > 1)
        base[...] = mine
        held[...] = result

        receive(bodies - 1)
        cross_receive(0)
        final = lax.dot_general(
            jnp.concatenate([forces[bodies - 1], cross_forces[0]], axis=1),
            last[...],
            (((1,), (1,)), ((), ())),
            preferred_element_type=jnp.float32,
        )
        residual[0] = base[...] - final[:, :narrow]
        change = final[:, wide : 2 * wide] + final[:, 2 * wide :]
        updated[0] = (held[...] - change)[:, :narrow]

    def sent(j):
        send(j).wait_send()

    loop(0, body, sent)
    loop(body + 1, bodies, sent)

    @pl.when(doubled)
    def _():
        cross_send().wait_send()

    slip_swap.wait_send()


def finish(updated, residual, updated_out, residual_out, sems):
    copies = [
        pltpu.make_async_copy(updated, updated_out, sems.at[0]),
        pltpu.make_async_copy(residual, residual_out, sems.at[1]),
    ]
    for copy in copies:
        copy.start()
    for copy in copies:
        copy.wait()


def stay(value):
    return pltpu.with_memory_space_constraint(value, pltpu.HBM)


def local(slip, inverse, positions):
    row_count = lax.axis_size("row")
    col_count = lax.axis_size("col")
    count = row_count * col_count
    bodies = count // 2
    blobs = positions.shape[2]
    rows, narrow = slip.shape[1:]
    wide = round_up(narrow, LANES)
    pad = round_up(blobs, CHUNK)
    vmem = pl.BlockSpec(memory_space=pltpu.VMEM)
    f32, bf16 = jnp.float32, jnp.bfloat16
    dma = pltpu.SemaphoreType.DMA
    extra = min(EXTRA, bodies // 2)
    tile_bytes = (bodies + extra) * 6 * pad * wide * 2
    updated, residual = pl.pallas_call(
        functools.partial(kernel, row_count, col_count, blobs, extra),
        out_shape=(
            pltpu.VMEM(slip.shape, f32),
            pltpu.VMEM(slip.shape, f32),
        ),
        in_specs=[pl.BlockSpec(memory_space=pltpu.HBM)] * 3,
        out_specs=(vmem, vmem),
        scratch_shapes=[
            pltpu.VMEM((rows, narrow), f32),
            pltpu.VMEM(inverse.shape[1:], f32),
            pltpu.VMEM((3, count, blobs), f32),
            pltpu.VMEM((2, wide, wide), bf16),
            pltpu.VMEM((2, wide, wide), bf16),
            pltpu.VMEM((bodies + extra, 2, 3 * pad, wide), bf16),
            pltpu.VMEM((8, LANES), f32),
            pltpu.VMEM((2, 4, pad, wide), f32),
            pltpu.VMEM((4, count, wide), f32),
            pltpu.VMEM((rows, narrow), f32),
            pltpu.VMEM((2, rows, wide), f32),
            pltpu.VMEM((2, rows, wide), f32),
            pltpu.VMEM((bodies, rows, wide), bf16),
            pltpu.VMEM((extra, rows, wide), bf16),
            pltpu.VMEM((rows, wide), f32),
            pltpu.VMEM((rows, narrow), f32),
            pltpu.VMEM((2, rows, wide), f32),
            pltpu.VMEM((2, wide, wide), bf16),
            pltpu.VMEM((3 * wide, 2 * wide), bf16),
            dma((3,)),
            dma((2,)),
            dma((2,)),
            dma((bodies,)),
            dma((bodies,)),
            dma((extra + 1,)),
            pltpu.SemaphoreType.REGULAR((2,)),
            pltpu.SemaphoreType.REGULAR((bodies,)),
        ],
        compiler_params=pltpu.CompilerParams(
            collective_id=0,
            has_side_effects=True,
            vmem_limit_bytes=min(tile_bytes + 16 * 2**20, 60 * 2**20),
        ),
    )(*(stay(v) for v in (slip, jnp.swapaxes(inverse, 0, 1), jnp.swapaxes(positions, 0, 1))))
    return pl.pallas_call(
        finish,
        out_shape=(jax.ShapeDtypeStruct(slip.shape, f32),) * 2,
        in_specs=[vmem, vmem],
        out_specs=(pl.BlockSpec(memory_space=pltpu.HBM),) * 2,
        scratch_shapes=[dma((2,))],
        compiler_params=pltpu.CompilerParams(vmem_limit_bytes=2**20),
    )(updated, residual)


def solution(mesh):
    in_specs = (
        P(("groups", "row", "col"), None, None),
        P(("groups", "row", "col"), None, None),
        P("groups", None, None),
    )
    out_specs = (P(("groups", "row", "col"), None, None), P(("groups", "row", "col"), None, None))
    return jax.shard_map(local, mesh=mesh, in_specs=in_specs, out_specs=out_specs, check_vma=False)
```

```python
import functools

import jax
import jax.numpy as jnp
from jax import lax
from jax.experimental import pallas as pl
from jax.experimental.pallas import tpu as pltpu
from jax.sharding import PartitionSpec as P

MESH = pl.DeviceIdType.MESH
LANES = 128
CHUNK = 16
EXTRA = 3


def round_up(value, step):
    return -(-value // step) * step


def split(value):
    high = value.astype(jnp.bfloat16)
    low = (value - high.astype(jnp.float32)).astype(jnp.bfloat16)
    return high, low


def kernel(
    row_count, col_count, blobs, extra,
    slip_hbm, inverse_hbm, positions_hbm,
    updated, residual,
    slip, inverse, positions,
    inv_high, inv_low, tiles, own_rows, own, source, other_slip, part, other_part,
    forces, cross_forces, held, base, far_part, turned, last,
    load_sems, slip_sems, part_sems, send_sems, recv_sems, cross_sems,
    go, ready,
):
    bodies = row_count * col_count // 2
    row = lax.axis_index("row")
    col = lax.axis_index("col")
    half = lax.rem(col, 2)
    partner = col + 1 - 2 * half
    body = (row * col_count + col) // 2
    narrow = 3 * blobs
    wide = inv_high.shape[-1]
    pad = own.shape[2]
    low_side = body < bodies // 2
    lead = body == 0

    def far(step):
        return jnp.where(low_side, bodies - 1 - step, step)

    def same(j):
        there = 2 * j + half
        return {"row": there // col_count, "col": lax.rem(there, col_count)}

    def cross(j):
        there = 2 * j + 1 - half
        return {"row": there // col_count, "col": lax.rem(there, col_count)}

    def loop(start, stop, action):
        def visit(j, carry):
            action(j)
            return carry

        lax.fori_loop(start, stop, visit, 0)

    def signal(sem, device):
        pl.semaphore_signal(sem, inc=1, device_id=device, device_id_type=MESH)

    barrier = pltpu.get_barrier_semaphore()

    @pl.when(half == 1)
    def _():
        signal(barrier, {"col": partner})

    loads = [
        pltpu.make_async_copy(inverse_hbm.at[:, 0, :], inverse, load_sems.at[0]),
        pltpu.make_async_copy(slip_hbm.at[0], slip, load_sems.at[1]),
        pltpu.make_async_copy(positions_hbm, positions, load_sems.at[2]),
    ]
    for load in loads:
        load.start()

    def swap(source_ref, target_ref, sems):
        return pltpu.make_async_remote_copy(
            src_ref=source_ref,
            dst_ref=target_ref,
            send_sem=sems.at[0],
            recv_sem=sems.at[1],
            device_id={"col": partner},
            device_id_type=MESH,
        )

    slip_swap = swap(slip_hbm.at[0], other_slip, slip_sems)

    def first(j):
        there = 2 * j
        return {"row": there // col_count, "col": lax.rem(there, col_count)}

    @pl.when(half == 0)
    def _():
        pl.semaphore_wait(barrier, jnp.where(lead, 1, 3))
        signal(go.at[0], {"col": partner})
        slip_swap.start()

    def greet(j):
        there = 2 * j + jnp.where(lead, 0, 1)
        signal(barrier, {"row": there // col_count, "col": lax.rem(there, col_count)})

    def others(action):
        loop(1, body, action)
        loop(body + 1, bodies, action)

    others(greet)

    @pl.when(half == 1)
    def _():
        pl.semaphore_wait(go.at[0], 1)
        slip_swap.start()

    @pl.when(jnp.logical_not(lead))
    def _():
        signal(ready.at[body], same(0))

    inv_high[...] = jnp.zeros_like(inv_high)
    inv_low[...] = jnp.zeros_like(inv_low)
    own_rows[...] = jnp.zeros_like(own_rows)

    def build(step, carry):
        j = step // 2
        t = lax.rem(step, 2)
        block = jnp.where(j < bodies, 2 * j + half, 2 * (2 * bodies - 1 - j) + 1 - half)
        lane = lax.broadcasted_iota(jnp.int32, (CHUNK, LANES), 1)
        there = [
            jnp.broadcast_to(source[a, pl.ds(block, 1), :], (CHUNK, LANES)) for a in range(3)
        ]

        def spread(parts, group):
            value = None
            for b, part_b in enumerate(parts):
                start = b * blobs - group * LANES
                if start >= LANES or start + blobs <= 0:
                    continue
                value = part_b if value is None else jnp.where(lane < start, value, part_b)
            return value

        for at in range(0, pad, CHUNK):
            d = [own[t, a, at : at + CHUNK, :] - there[a] for a in range(3)]
            dist_sq = d[0] * d[0] + d[1] * d[1] + d[2] * d[2]
            r = lax.rsqrt(jnp.where(dist_sq > 0.0, dist_sq, 1.0))
            r2 = r * r
            k = 0.75 * r
            u = k * r2
            apart = dist_sq >= 4.0
            isotropic = jnp.where(
                apart, k + (2.0 / 3.0) * u, 1.0 - (9.0 / 32.0) * (dist_sq * r)
            )
            anisotropic = jnp.where(apart, u - (2.0 * u) * r2, (3.0 / 32.0) * r)
            scaled = [anisotropic * da for da in d]
            for a in range(3):
                parts = []
                for b in range(3):
                    value = scaled[min(a, b)] * d[max(a, b)]
                    if a == b:
                        value = value + isotropic
                    shift = b * blobs % LANES
                    parts.append(pltpu.roll(value, shift, 1) if shift else value)
                for group in range(wide // LANES):
                    tiles[
                        j,
                        t,
                        a * pad + at : a * pad + at + CHUNK,
                        group * LANES : (group + 1) * LANES,
                    ] = spread(parts, group).astype(jnp.bfloat16)
        return carry

    def apply(values, h):
        high, low = split(jnp.pad(values, ((0, 0), (0, wide - narrow))))
        big = inv_high[h]
        small = inv_low[h]
        rows = values.shape[0]
        both = jnp.dot(
            jnp.concatenate([high, low], axis=0), big, preferred_element_type=jnp.float32
        )
        cross = jnp.dot(high, small, preferred_element_type=jnp.float32)
        return both[:rows] + (both[rows:] + cross)

    loads[0].wait()
    for h in range(2):
        high, low = split(inverse[h * narrow : (h + 1) * narrow, :])
        inv_high[h, :narrow, :narrow] = high
        inv_low[h, :narrow, :narrow] = low
    loads[1].wait()
    force = apply(slip[...], half)
    slip_swap.wait_recv()
    force = force + apply(other_slip[...], 1 - half)
    forces[body] = force.astype(jnp.bfloat16)
    held[...] = force

    def send(j):
        return pltpu.make_async_remote_copy(
            src_ref=forces.at[body],
            dst_ref=forces.at[body],
            send_sem=send_sems.at[j],
            recv_sem=recv_sems.at[body],
            device_id=same(j),
            device_id_type=MESH,
        )

    slot = bodies - 1 - body
    doubled = (slot < extra) & jnp.logical_not(lead)

    def cross_send():
        return pltpu.make_async_remote_copy(
            src_ref=forces.at[body],
            dst_ref=cross_forces.at[slot],
            send_sem=cross_sems.at[extra],
            recv_sem=cross_sems.at[slot],
            device_id=cross(0),
            device_id_type=MESH,
        )

    @pl.when(jnp.logical_not(lead))
    def _():
        send(0).start()

    @pl.when(doubled)
    def _():
        cross_send().start()

    if bodies > 2:

        @pl.when(jnp.logical_not(lead) & (half == 1))
        def _():
            pl.semaphore_wait(barrier, 2 * (bodies - 2))
            signal(go.at[1], {"col": partner})

        @pl.when(jnp.logical_not(lead) & (half == 0))
        def _():
            pl.semaphore_wait(go.at[1], 1)

    @pl.when(jnp.logical_not(lead))
    def _():
        others(lambda j: send(j).start())

    loads[2].wait()
    for a in range(3):
        source[a] = jnp.pad(positions[a], ((0, 0), (0, LANES - blobs)))
        for t in range(2):
            own_rows[3 * t + a : 3 * t + a + 1, :blobs] = positions[a, pl.ds(2 * body + t, 1), :]
    own_cols = own_rows[...].T
    for t in range(2):
        for a in range(3):
            own[t, a] = jnp.broadcast_to(
                own_cols[:pad, 3 * t + a : 3 * t + a + 1], (pad, LANES)
            )

    lax.fori_loop(0, jnp.where(lead, 2 * (bodies + extra), 2 * bodies), build, 0)

    def send_on(j):
        pl.semaphore_wait(ready.at[j], 1)
        send(j).start()

    @pl.when(lead)
    def _():
        loop(1, bodies, send_on)

    def product(values, j):
        return lax.dot_general(
            values,
            tiles[j].reshape(6 * pad, wide),
            (((1,), (1,)), ((), ())),
            preferred_element_type=jnp.float32,
        )

    def receive(j):
        pltpu.make_async_remote_copy(
            src_ref=forces.at[j],
            dst_ref=forces.at[j],
            send_sem=send_sems.at[0],
            recv_sem=recv_sems.at[j],
            device_id={"col": partner},
            device_id_type=MESH,
        ).wait_recv()

    def cross_receive(f):
        pltpu.make_async_remote_copy(
            src_ref=cross_forces.at[f],
            dst_ref=cross_forces.at[f],
            send_sem=cross_sems.at[extra],
            recv_sem=cross_sems.at[f],
            device_id={"col": partner},
            device_id_type=MESH,
        ).wait_recv()

    def gather(picks):
        for j in picks:

            @pl.when(j != body)
            def _(j=j):
                receive(j)

        total = product(forces[picks[0]], picks[0])
        for j in picks[1:]:
            total = total + product(forces[j], j)
        return total

    def gather_run(start, stop):
        if stop - start <= 8:
            size = (stop - start + 1) // 2
            total = gather([far(bodies - 1 - k) for k in range(start, start + size)])
            return total + gather([far(bodies - 1 - k) for k in range(start + size, stop)])
        return lax.fori_loop(
            start,
            stop,
            lambda k, total: total + gather([far(bodies - 1 - k)]),
            jnp.zeros((slip.shape[0], 6 * pad), jnp.float32),
        )

    def compact(total):
        full = round_up(6 * pad, LANES)
        total = jnp.pad(total, ((0, 0), (0, full - 6 * pad)))
        lane = lax.broadcasted_iota(jnp.int32, total.shape, 1)

        def moved(by):
            return pltpu.roll(total, full - by, 1) if by else total

        values = []
        for t in range(2):
            start = 3 * t * pad
            shift = pad - blobs
            value = jnp.where(
                lane < blobs,
                moved(start),
                jnp.where(lane < 2 * blobs, moved(start + shift), moved(start + 2 * shift)),
            )
            values.append(value[:, :wide])
        return values

    part_swap = swap(part, other_part, part_sems)

    def share(total):
        for t, value in enumerate(compact(total)):
            part[t] = value
        part_swap.start()

    def settle(more):
        part_swap.wait()
        sums = [part[t] + other_part[t] for t in (half, 1 - half)]
        if more:
            sums = [value + far_part[t] for value, t in zip(sums, (half, 1 - half))]
        mine = slip[...] - sums[0][:, :narrow]
        theirs = other_slip[...] - sums[1][:, :narrow]
        return mine, held[...] + (apply(mine, half) + apply(theirs, 1 - half))

    @pl.when(jnp.logical_not(lead))
    def _():
        share(gather_run(0, bodies))
        mine, result = settle(False)
        residual[0] = mine
        updated[0] = result[:, :narrow]

    @pl.when(lead)
    def _():
        row_at = lax.broadcasted_iota(jnp.int32, (wide, 3 * pad), 0)
        col_at = lax.broadcasted_iota(jnp.int32, (wide, 3 * pad), 1)
        gap = pad - blobs
        wanted = row_at + jnp.where(row_at < blobs, 0, jnp.where(row_at < 2 * blobs, gap, 2 * gap))
        picked = jnp.where((col_at == wanted) & (row_at < narrow), 1.0, 0.0).astype(jnp.bfloat16)
        for s, block in enumerate((bodies - 1, bodies)):
            lanes = slice(s * wide, (s + 1) * wide)
            folded = jnp.zeros((wide, wide), jnp.float32)
            for t in range(2):
                tight = jnp.dot(picked, tiles[block, t], preferred_element_type=jnp.float32)
                tight = tight.astype(jnp.bfloat16)
                turned[t] = tight
                for side in (inv_high, inv_low):
                    folded = folded + lax.dot_general(
                        side[t], tight, (((0,), (0,)), ((), ())), preferred_element_type=jnp.float32
                    )
            high, low = split(folded)
            last[:wide, lanes] = turned[half]
            last[wide : 2 * wide, lanes] = high
            last[2 * wide :, lanes] = low

        share(gather_run(0, bodies - extra))

        if extra > 1:
            for f in range(1, extra):
                receive(bodies - 1 - f)
                cross_receive(f)
            total = jnp.zeros((slip.shape[0], 6 * pad), jnp.float32)
            for f in range(1, extra):
                total = total + product(forces[bodies - 1 - f], bodies - 1 - f)
                total = total + product(cross_forces[f], bodies + f)
            for t, value in enumerate(compact(total)):
                far_part[t] = value

        mine, result = settle(extra > 1)
        base[...] = mine
        held[...] = result

        receive(bodies - 1)
        cross_receive(0)
        final = lax.dot_general(
            jnp.concatenate([forces[bodies - 1], cross_forces[0]], axis=1),
            last[...],
            (((1,), (1,)), ((), ())),
            preferred_element_type=jnp.float32,
        )
        residual[0] = base[...] - final[:, :narrow]
        change = final[:, wide : 2 * wide] + final[:, 2 * wide :]
        updated[0] = (held[...] - change)[:, :narrow]

    def sent(j):
        send(j).wait_send()

    loop(0, body, sent)
    loop(body + 1, bodies, sent)

    @pl.when(doubled)
    def _():
        cross_send().wait_send()

    slip_swap.wait_send()


def finish(updated, residual, updated_out, residual_out, sems):
    copies = [
        pltpu.make_async_copy(updated, updated_out, sems.at[0]),
        pltpu.make_async_copy(residual, residual_out, sems.at[1]),
    ]
    for copy in copies:
        copy.start()
    for copy in copies:
        copy.wait()


def stay(value):
    return pltpu.with_memory_space_constraint(value, pltpu.HBM)


def local(slip, inverse, positions):
    row_count = lax.axis_size("row")
    col_count = lax.axis_size("col")
    count = row_count * col_count
    bodies = count // 2
    blobs = positions.shape[2]
    rows, narrow = slip.shape[1:]
    wide = round_up(narrow, LANES)
    pad = round_up(blobs, CHUNK)
    vmem = pl.BlockSpec(memory_space=pltpu.VMEM)
    f32, bf16 = jnp.float32, jnp.bfloat16
    dma = pltpu.SemaphoreType.DMA
    extra = min(EXTRA, bodies // 2)
    tile_bytes = (bodies + extra) * 6 * pad * wide * 2
    updated, residual = pl.pallas_call(
        functools.partial(kernel, row_count, col_count, blobs, extra),
        out_shape=(
            pltpu.VMEM(slip.shape, f32),
            pltpu.VMEM(slip.shape, f32),
        ),
        in_specs=[pl.BlockSpec(memory_space=pltpu.HBM)] * 3,
        out_specs=(vmem, vmem),
        scratch_shapes=[
            pltpu.VMEM((rows, narrow), f32),
            pltpu.VMEM(inverse.shape[1:], f32),
            pltpu.VMEM((3, count, blobs), f32),
            pltpu.VMEM((2, wide, wide), bf16),
            pltpu.VMEM((2, wide, wide), bf16),
            pltpu.VMEM((bodies + extra, 2, 3 * pad, wide), bf16),
            pltpu.VMEM((8, LANES), f32),
            pltpu.VMEM((2, 3, pad, LANES), f32),
            pltpu.VMEM((3, count, LANES), f32),
            pltpu.VMEM((rows, narrow), f32),
            pltpu.VMEM((2, rows, wide), f32),
            pltpu.VMEM((2, rows, wide), f32),
            pltpu.VMEM((bodies, rows, wide), bf16),
            pltpu.VMEM((extra, rows, wide), bf16),
            pltpu.VMEM((rows, wide), f32),
            pltpu.VMEM((rows, narrow), f32),
            pltpu.VMEM((2, rows, wide), f32),
            pltpu.VMEM((2, wide, wide), bf16),
            pltpu.VMEM((3 * wide, 2 * wide), bf16),
            dma((3,)),
            dma((2,)),
            dma((2,)),
            dma((bodies,)),
            dma((bodies,)),
            dma((extra + 1,)),
            pltpu.SemaphoreType.REGULAR((2,)),
            pltpu.SemaphoreType.REGULAR((bodies,)),
        ],
        compiler_params=pltpu.CompilerParams(
            collective_id=0,
            has_side_effects=True,
            vmem_limit_bytes=min(tile_bytes + 16 * 2**20, 60 * 2**20),
        ),
    )(*(stay(v) for v in (slip, jnp.swapaxes(inverse, 0, 1), jnp.swapaxes(positions, 0, 1))))
    return pl.pallas_call(
        finish,
        out_shape=(jax.ShapeDtypeStruct(slip.shape, f32),) * 2,
        in_specs=[vmem, vmem],
        out_specs=(pl.BlockSpec(memory_space=pltpu.HBM),) * 2,
        scratch_shapes=[dma((2,))],
        compiler_params=pltpu.CompilerParams(vmem_limit_bytes=2**20),
    )(updated, residual)


def solution(mesh):
    in_specs = (
        P(("groups", "row", "col"), None, None),
        P(("groups", "row", "col"), None, None),
        P("groups", None, None),
    )
    out_specs = (P(("groups", "row", "col"), None, None), P(("groups", "row", "col"), None, None))
    return jax.shard_map(local, mesh=mesh, in_specs=in_specs, out_specs=out_specs, check_vma=False)
```

```python
import functools

import jax
import jax.numpy as jnp
from jax import lax
from jax.experimental import pallas as pl
from jax.experimental.pallas import tpu as pltpu
from jax.sharding import PartitionSpec as P

MESH = pl.DeviceIdType.MESH
LANES = 128
CHUNK = 16
EXTRA = 3


def round_up(value, step):
    return -(-value // step) * step


def split(value):
    high = value.astype(jnp.bfloat16)
    low = (value - high.astype(jnp.float32)).astype(jnp.bfloat16)
    return high, low


def kernel(
    row_count, col_count, blobs, extra,
    slip_hbm, inverse_hbm, positions_hbm,
    updated, residual,
    slip, inverse, positions,
    inv_high, inv_low, tiles, own_rows, own, source, other_slip, part, other_part,
    forces, twin_forces, held, base, far_part, turned, last,
    load_sems, slip_sems, part_sems, send_sems, recv_sems, twin_sems,
    go, ready,
):
    bodies = row_count * col_count // 2
    row = lax.axis_index("row")
    col = lax.axis_index("col")
    half = lax.rem(col, 2)
    partner = col + 1 - 2 * half
    body = (row * col_count + col) // 2
    narrow = 3 * blobs
    wide = inv_high.shape[-1]
    pad = own.shape[2]
    low_side = body < bodies // 2
    lead = body == 0

    def far(step):
        return jnp.where(low_side, bodies - 1 - step, step)

    def same(j):
        there = 2 * j + half
        return {"row": there // col_count, "col": lax.rem(there, col_count)}

    def cross(j):
        there = 2 * j + 1 - half
        return {"row": there // col_count, "col": lax.rem(there, col_count)}

    def loop(start, stop, action):
        def visit(j, carry):
            action(j)
            return carry

        lax.fori_loop(start, stop, visit, 0)

    def signal(sem, device):
        pl.semaphore_signal(sem, inc=1, device_id=device, device_id_type=MESH)

    barrier = pltpu.get_barrier_semaphore()

    def swap(source_ref, target_ref, sems):
        return pltpu.make_async_remote_copy(
            src_ref=source_ref,
            dst_ref=target_ref,
            send_sem=sems.at[0],
            recv_sem=sems.at[1],
            device_id={"col": partner},
            device_id_type=MESH,
        )

    slip_swap = swap(slip_hbm.at[0], other_slip, slip_sems)

    @pl.when(half == 1)
    def _():
        signal(barrier, {"col": partner})

    @pl.when(half == 0)
    def _():
        pl.semaphore_wait(barrier, jnp.where(lead, 1, 3))
        signal(go.at[0], {"col": partner})
        slip_swap.start()

    loads = [
        pltpu.make_async_copy(inverse_hbm.at[:, 0, :], inverse, load_sems.at[0]),
        pltpu.make_async_copy(slip_hbm.at[0], slip, load_sems.at[1]),
        pltpu.make_async_copy(positions_hbm, positions, load_sems.at[2]),
    ]
    for load in (loads[1], loads[0], loads[2]):
        load.start()

    def greet(j):
        there = 2 * j + jnp.where(lead, 0, 1)
        signal(barrier, {"row": there // col_count, "col": lax.rem(there, col_count)})

    def others(action):
        loop(1, body, action)
        loop(body + 1, bodies, action)

    others(greet)

    @pl.when(half == 1)
    def _():
        loads[1].wait()
        pl.semaphore_wait(go.at[0], 1)
        swap(slip, other_slip, slip_sems).start()

    @pl.when(jnp.logical_not(lead))
    def _():
        signal(ready.at[body], cross(0))

    inv_high[...] = jnp.zeros_like(inv_high)
    inv_low[...] = jnp.zeros_like(inv_low)
    own_rows[...] = jnp.zeros_like(own_rows)

    def build(step, carry):
        j = step
        here = jnp.where(j == body, half, 1 - half)
        block = jnp.where(j < bodies, 2 * j + here, 2 * (2 * bodies - 1 - j) + half)
        lane = lax.broadcasted_iota(jnp.int32, (CHUNK, LANES), 1)
        there = [
            jnp.broadcast_to(source[a, pl.ds(block, 1), :], (CHUNK, LANES)) for a in range(3)
        ]

        def spread(parts, group):
            value = None
            for b, part_b in enumerate(parts):
                start = b * blobs - group * LANES
                if start >= LANES or start + blobs <= 0:
                    continue
                value = part_b if value is None else jnp.where(lane < start, value, part_b)
            return value

        for t, at in [(t, at) for at in range(0, pad, CHUNK) for t in range(2)]:
            d = [own[t, a, at : at + CHUNK, :] - there[a] for a in range(3)]
            dist_sq = d[0] * d[0] + d[1] * d[1] + d[2] * d[2]
            r = lax.rsqrt(jnp.where(dist_sq > 0.0, dist_sq, 1.0))
            r2 = r * r
            k = 0.75 * r
            u = k * r2
            apart = dist_sq >= 4.0
            isotropic = jnp.where(
                apart, k + (2.0 / 3.0) * u, 1.0 - (9.0 / 32.0) * (dist_sq * r)
            )
            anisotropic = jnp.where(apart, u - (2.0 * u) * r2, (3.0 / 32.0) * r)
            scaled = [anisotropic * da for da in d]
            for a in range(3):
                parts = []
                for b in range(3):
                    value = scaled[min(a, b)] * d[max(a, b)]
                    if a == b:
                        value = value + isotropic
                    shift = b * blobs % LANES
                    parts.append(pltpu.roll(value, shift, 1) if shift else value)
                for group in range(wide // LANES):
                    tiles[
                        j,
                        t,
                        a * pad + at : a * pad + at + CHUNK,
                        group * LANES : (group + 1) * LANES,
                    ] = spread(parts, group).astype(jnp.bfloat16)
        return carry

    def apply(values, h):
        high, low = split(jnp.pad(values, ((0, 0), (0, wide - narrow))))
        big = inv_high[h]
        small = inv_low[h]
        rows = values.shape[0]
        both = jnp.dot(
            jnp.concatenate([high, low], axis=0), big, preferred_element_type=jnp.float32
        )
        cross = jnp.dot(high, small, preferred_element_type=jnp.float32)
        return both[:rows] + (both[rows:] + cross)

    loads[0].wait()
    for h in range(2):
        high, low = split(inverse[h * narrow : (h + 1) * narrow, :])
        inv_high[h, :narrow, :narrow] = high
        inv_low[h, :narrow, :narrow] = low
    @pl.when(half == 0)
    def _():
        loads[1].wait()

    force = apply(slip[...], half)
    slip_swap.wait_recv()
    force = force + apply(other_slip[...], 1 - half)
    forces[body] = force.astype(jnp.bfloat16)
    held[...] = force

    def send(j):
        return pltpu.make_async_remote_copy(
            src_ref=forces.at[body],
            dst_ref=forces.at[body],
            send_sem=send_sems.at[j],
            recv_sem=recv_sems.at[body],
            device_id=cross(j),
            device_id_type=MESH,
        )

    slot = bodies - 1 - body
    doubled = (slot < extra) & jnp.logical_not(lead)

    def twin_send():
        return pltpu.make_async_remote_copy(
            src_ref=forces.at[body],
            dst_ref=twin_forces.at[slot],
            send_sem=twin_sems.at[extra],
            recv_sem=twin_sems.at[slot],
            device_id=same(0),
            device_id_type=MESH,
        )

    @pl.when(jnp.logical_not(lead))
    def _():
        send(0).start()

    @pl.when(doubled)
    def _():
        twin_send().start()

    if bodies > 2:

        @pl.when(jnp.logical_not(lead) & (half == 1))
        def _():
            pl.semaphore_wait(barrier, 2 * (bodies - 2))
            signal(go.at[1], {"col": partner})

        @pl.when(jnp.logical_not(lead) & (half == 0))
        def _():
            pl.semaphore_wait(go.at[1], 1)

    @pl.when(jnp.logical_not(lead))
    def _():
        others(lambda j: send(j).start())

    loads[2].wait()
    for a in range(3):
        source[a] = jnp.pad(positions[a], ((0, 0), (0, LANES - blobs)))
        for t in range(2):
            own_rows[3 * t + a : 3 * t + a + 1, :blobs] = positions[a, pl.ds(2 * body + t, 1), :]
    own_cols = own_rows[...].T
    for t in range(2):
        for a in range(3):
            own[t, a] = jnp.broadcast_to(
                own_cols[:pad, 3 * t + a : 3 * t + a + 1], (pad, LANES)
            )

    lax.fori_loop(0, jnp.where(lead, bodies + extra, bodies), build, 0)

    def send_on(j):
        pl.semaphore_wait(ready.at[j], 1)
        send(j).start()

    @pl.when(lead)
    def _():
        loop(1, bodies, send_on)

    def product(values, j):
        return lax.dot_general(
            values,
            tiles[j].reshape(6 * pad, wide),
            (((1,), (1,)), ((), ())),
            preferred_element_type=jnp.float32,
        )

    def receive(j):
        pltpu.make_async_remote_copy(
            src_ref=forces.at[j],
            dst_ref=forces.at[j],
            send_sem=send_sems.at[0],
            recv_sem=recv_sems.at[j],
            device_id={"col": partner},
            device_id_type=MESH,
        ).wait_recv()

    def twin_receive(f):
        pltpu.make_async_remote_copy(
            src_ref=twin_forces.at[f],
            dst_ref=twin_forces.at[f],
            send_sem=twin_sems.at[extra],
            recv_sem=twin_sems.at[f],
            device_id={"col": partner},
            device_id_type=MESH,
        ).wait_recv()

    def gather(picks):
        for j in picks:

            @pl.when(j != body)
            def _(j=j):
                receive(j)

        total = product(forces[picks[0]], picks[0])
        for j in picks[1:]:
            total = total + product(forces[j], j)
        return total

    def gather_run(start, stop):
        if stop - start <= 8:
            size = (stop - start + 1) // 2
            total = gather([far(bodies - 1 - k) for k in range(start, start + size)])
            return total + gather([far(bodies - 1 - k) for k in range(start + size, stop)])
        return lax.fori_loop(
            start,
            stop,
            lambda k, total: total + gather([far(bodies - 1 - k)]),
            jnp.zeros((slip.shape[0], 6 * pad), jnp.float32),
        )

    def compact(total):
        full = round_up(6 * pad, LANES)
        total = jnp.pad(total, ((0, 0), (0, full - 6 * pad)))
        lane = lax.broadcasted_iota(jnp.int32, total.shape, 1)

        def moved(by):
            return pltpu.roll(total, full - by, 1) if by else total

        values = []
        for t in range(2):
            start = 3 * t * pad
            shift = pad - blobs
            value = jnp.where(
                lane < blobs,
                moved(start),
                jnp.where(lane < 2 * blobs, moved(start + shift), moved(start + 2 * shift)),
            )
            values.append(value[:, :wide])
        return values

    part_swap = swap(part, other_part, part_sems)

    def share(total):
        for t, value in enumerate(compact(total)):
            part[t] = value
        part_swap.start()

    def settle(more):
        part_swap.wait()
        sums = [part[t] + other_part[t] for t in (half, 1 - half)]
        if more:
            sums = [value + far_part[t] for value, t in zip(sums, (half, 1 - half))]
        mine = slip[...] - sums[0][:, :narrow]
        theirs = other_slip[...] - sums[1][:, :narrow]
        return mine, held[...] + (apply(mine, half) + apply(theirs, 1 - half))

    @pl.when(jnp.logical_not(lead))
    def _():
        share(gather_run(0, bodies))
        mine, result = settle(False)
        residual[0] = mine
        updated[0] = result[:, :narrow]

    @pl.when(lead)
    def _():
        row_at = lax.broadcasted_iota(jnp.int32, (wide, 3 * pad), 0)
        col_at = lax.broadcasted_iota(jnp.int32, (wide, 3 * pad), 1)
        gap = pad - blobs
        wanted = row_at + jnp.where(row_at < blobs, 0, jnp.where(row_at < 2 * blobs, gap, 2 * gap))
        picked = jnp.where((col_at == wanted) & (row_at < narrow), 1.0, 0.0).astype(jnp.bfloat16)
        for s, block in enumerate((bodies - 1, bodies)):
            rows = slice(s * wide, (s + 1) * wide)
            folded = jnp.zeros((wide, wide), jnp.float32)
            for t in range(2):
                tight = lax.dot_general(
                    tiles[block, t],
                    picked,
                    (((0,), (1,)), ((), ())),
                    preferred_element_type=jnp.float32,
                ).astype(jnp.bfloat16)
                turned[t] = tight
                for side in (inv_high, inv_low):
                    folded = folded + jnp.dot(tight, side[t], preferred_element_type=jnp.float32)
            high, low = split(folded)
            last[rows, :wide] = turned[half]
            last[rows, wide : 2 * wide] = high
            last[rows, 2 * wide :] = low

        share(gather_run(0, bodies - extra))

        if extra > 1:
            for f in range(1, extra):
                receive(bodies - 1 - f)
                twin_receive(f)
            total = jnp.zeros((slip.shape[0], 6 * pad), jnp.float32)
            for f in range(1, extra):
                total = total + product(forces[bodies - 1 - f], bodies - 1 - f)
                total = total + product(twin_forces[f], bodies + f)
            for t, value in enumerate(compact(total)):
                far_part[t] = value

        mine, result = settle(extra > 1)
        base[...] = mine
        held[...] = result

        receive(bodies - 1)
        twin_receive(0)
        final = jnp.dot(
            jnp.concatenate([forces[bodies - 1], twin_forces[0]], axis=1),
            last[...],
            preferred_element_type=jnp.float32,
        )
        residual[0] = base[...] - final[:, :narrow]
        change = final[:, wide : 2 * wide] + final[:, 2 * wide :]
        updated[0] = (held[...] - change)[:, :narrow]

    def sent(j):
        send(j).wait_send()

    loop(0, body, sent)
    loop(body + 1, bodies, sent)

    @pl.when(doubled)
    def _():
        twin_send().wait_send()

    slip_swap.wait_send()


def finish(updated, residual, updated_out, residual_out, sems):
    copies = [
        pltpu.make_async_copy(updated, updated_out, sems.at[0]),
        pltpu.make_async_copy(residual, residual_out, sems.at[1]),
    ]
    for copy in copies:
        copy.start()
    for copy in copies:
        copy.wait()


def stay(value):
    return pltpu.with_memory_space_constraint(value, pltpu.HBM)


def local(slip, inverse, positions):
    row_count = lax.axis_size("row")
    col_count = lax.axis_size("col")
    count = row_count * col_count
    bodies = count // 2
    blobs = positions.shape[2]
    rows, narrow = slip.shape[1:]
    wide = round_up(narrow, LANES)
    pad = round_up(blobs, CHUNK)
    vmem = pl.BlockSpec(memory_space=pltpu.VMEM)
    f32, bf16 = jnp.float32, jnp.bfloat16
    dma = pltpu.SemaphoreType.DMA
    extra = min(EXTRA, bodies // 2)
    tile_bytes = (bodies + extra) * 6 * pad * wide * 2
    updated, residual = pl.pallas_call(
        functools.partial(kernel, row_count, col_count, blobs, extra),
        out_shape=(
            pltpu.VMEM(slip.shape, f32),
            pltpu.VMEM(slip.shape, f32),
        ),
        in_specs=[pl.BlockSpec(memory_space=pltpu.HBM)] * 3,
        out_specs=(vmem, vmem),
        scratch_shapes=[
            pltpu.VMEM((rows, narrow), f32),
            pltpu.VMEM(inverse.shape[1:], f32),
            pltpu.VMEM((3, count, blobs), f32),
            pltpu.VMEM((2, wide, wide), bf16),
            pltpu.VMEM((2, wide, wide), bf16),
            pltpu.VMEM((bodies + extra, 2, 3 * pad, wide), bf16),
            pltpu.VMEM((8, LANES), f32),
            pltpu.VMEM((2, 3, pad, LANES), f32),
            pltpu.VMEM((3, count, LANES), f32),
            pltpu.VMEM((rows, narrow), f32),
            pltpu.VMEM((2, rows, wide), f32),
            pltpu.VMEM((2, rows, wide), f32),
            pltpu.VMEM((bodies, rows, wide), bf16),
            pltpu.VMEM((extra, rows, wide), bf16),
            pltpu.VMEM((rows, wide), f32),
            pltpu.VMEM((rows, narrow), f32),
            pltpu.VMEM((2, rows, wide), f32),
            pltpu.VMEM((2, wide, wide), bf16),
            pltpu.VMEM((2 * wide, 3 * wide), bf16),
            dma((3,)),
            dma((2,)),
            dma((2,)),
            dma((bodies,)),
            dma((bodies,)),
            dma((extra + 1,)),
            pltpu.SemaphoreType.REGULAR((2,)),
            pltpu.SemaphoreType.REGULAR((bodies,)),
        ],
        compiler_params=pltpu.CompilerParams(
            collective_id=0,
            has_side_effects=True,
            vmem_limit_bytes=min(tile_bytes + 16 * 2**20, 60 * 2**20),
        ),
    )(*(stay(v) for v in (slip, jnp.swapaxes(inverse, 0, 1), jnp.swapaxes(positions, 0, 1))))
    return pl.pallas_call(
        finish,
        out_shape=(jax.ShapeDtypeStruct(slip.shape, f32),) * 2,
        in_specs=[vmem, vmem],
        out_specs=(pl.BlockSpec(memory_space=pltpu.HBM),) * 2,
        scratch_shapes=[dma((2,))],
        compiler_params=pltpu.CompilerParams(vmem_limit_bytes=2**20),
    )(updated, residual)


def solution(mesh):
    in_specs = (
        P(("groups", "row", "col"), None, None),
        P(("groups", "row", "col"), None, None),
        P("groups", None, None),
    )
    out_specs = (P(("groups", "row", "col"), None, None), P(("groups", "row", "col"), None, None))
    return jax.shard_map(local, mesh=mesh, in_specs=in_specs, out_specs=out_specs, check_vma=False)
```

```python
import functools

import jax
import jax.numpy as jnp
from jax import lax
from jax.experimental import pallas as pl
from jax.experimental.pallas import tpu as pltpu
from jax.sharding import PartitionSpec as P

MESH = pl.DeviceIdType.MESH
LANES = 128
CHUNK = 16
EXTRA = 3


def round_up(value, step):
    return -(-value // step) * step


def split(value):
    high = value.astype(jnp.bfloat16)
    low = (value - high.astype(jnp.float32)).astype(jnp.bfloat16)
    return high, low


def kernel(
    row_count, col_count, blobs, extra,
    slip_hbm, inverse_hbm, positions_hbm,
    updated, residual,
    slip, inverse, positions,
    inv_high, inv_low, tiles, own_rows, own, source, other_slip, part, other_part,
    forces, twin_forces, held, base, far_part, turned, last,
    load_sems, slip_sems, part_sems, send_sems, recv_sems, twin_sems,
    go, ready,
):
    bodies = row_count * col_count // 2
    row = lax.axis_index("row")
    col = lax.axis_index("col")
    half = lax.rem(col, 2)
    partner = col + 1 - 2 * half
    body = (row * col_count + col) // 2
    narrow = 3 * blobs
    wide = inv_high.shape[-1]
    pad = own.shape[2]
    low_side = body < bodies // 2
    lead = body == 0

    def far(step):
        return jnp.where(low_side, bodies - 1 - step, step)

    def same(j):
        there = 2 * j + half
        return {"row": there // col_count, "col": lax.rem(there, col_count)}

    def cross(j):
        there = 2 * j + 1 - half
        return {"row": there // col_count, "col": lax.rem(there, col_count)}

    def loop(start, stop, action):
        def visit(j, carry):
            action(j)
            return carry

        lax.fori_loop(start, stop, visit, 0)

    def signal(sem, device):
        pl.semaphore_signal(sem, inc=1, device_id=device, device_id_type=MESH)

    barrier = pltpu.get_barrier_semaphore()

    def swap(source_ref, target_ref, sems):
        return pltpu.make_async_remote_copy(
            src_ref=source_ref,
            dst_ref=target_ref,
            send_sem=sems.at[0],
            recv_sem=sems.at[1],
            device_id={"col": partner},
            device_id_type=MESH,
        )

    slip_swap = swap(slip_hbm.at[0], other_slip, slip_sems)

    @pl.when(half == 1)
    def _():
        signal(barrier, {"col": partner})

    @pl.when(half == 0)
    def _():
        pl.semaphore_wait(barrier, jnp.where(lead, 1, 3))
        signal(go.at[0], {"col": partner})
        slip_swap.start()

    loads = [
        pltpu.make_async_copy(slip_hbm.at[0], slip, load_sems.at[0]),
        pltpu.make_async_copy(positions_hbm, positions, load_sems.at[1]),
    ]
    fetches = [
        pltpu.make_async_copy(
            inverse_hbm.at[pl.ds(h * narrow, narrow), 0, :], inverse.at[h], load_sems.at[2 + k]
        )
        for k, h in enumerate((half, 1 - half))
    ]
    for load in (loads[0], *fetches, loads[1]):
        load.start()

    def greet(j):
        there = 2 * j + jnp.where(lead, 0, 1)
        signal(barrier, {"row": there // col_count, "col": lax.rem(there, col_count)})

    def others(action):
        loop(1, body, action)
        loop(body + 1, bodies, action)

    others(greet)

    @pl.when(half == 1)
    def _():
        loads[0].wait()
        pl.semaphore_wait(go.at[0], 1)
        swap(slip, other_slip, slip_sems).start()

    @pl.when(jnp.logical_not(lead))
    def _():
        signal(ready.at[body], cross(0))

    inv_high[...] = jnp.zeros_like(inv_high)
    inv_low[...] = jnp.zeros_like(inv_low)
    own_rows[...] = jnp.zeros_like(own_rows)

    def build(step, carry):
        j = step
        here = jnp.where(j == body, half, 1 - half)
        block = jnp.where(j < bodies, 2 * j + here, 2 * (2 * bodies - 1 - j) + half)
        lane = lax.broadcasted_iota(jnp.int32, (CHUNK, LANES), 1)
        there = [
            jnp.broadcast_to(source[a, pl.ds(block, 1), :], (CHUNK, LANES)) for a in range(3)
        ]

        def spread(parts, group):
            value = None
            for b, part_b in enumerate(parts):
                start = b * blobs - group * LANES
                if start >= LANES or start + blobs <= 0:
                    continue
                value = part_b if value is None else jnp.where(lane < start, value, part_b)
            return value

        for t, at in [(t, at) for at in range(0, pad, CHUNK) for t in range(2)]:
            d = [own[t, a, at : at + CHUNK, :] - there[a] for a in range(3)]
            dist_sq = d[0] * d[0] + d[1] * d[1] + d[2] * d[2]
            r = lax.rsqrt(jnp.where(dist_sq > 0.0, dist_sq, 1.0))
            r2 = r * r
            k = 0.75 * r
            u = k * r2
            apart = dist_sq >= 4.0
            isotropic = jnp.where(
                apart, k + (2.0 / 3.0) * u, 1.0 - (9.0 / 32.0) * (dist_sq * r)
            )
            anisotropic = jnp.where(apart, u - (2.0 * u) * r2, (3.0 / 32.0) * r)
            scaled = [anisotropic * da for da in d]
            for a in range(3):
                parts = []
                for b in range(3):
                    value = scaled[min(a, b)] * d[max(a, b)]
                    if a == b:
                        value = value + isotropic
                    shift = b * blobs % LANES
                    parts.append(pltpu.roll(value, shift, 1) if shift else value)
                for group in range(wide // LANES):
                    tiles[
                        j,
                        t,
                        a * pad + at : a * pad + at + CHUNK,
                        group * LANES : (group + 1) * LANES,
                    ] = spread(parts, group).astype(jnp.bfloat16)
        return carry

    def apply(values, h):
        high, low = split(jnp.pad(values, ((0, 0), (0, wide - narrow))))
        big = inv_high[h]
        small = inv_low[h]
        rows = values.shape[0]
        both = jnp.dot(
            jnp.concatenate([high, low], axis=0), big, preferred_element_type=jnp.float32
        )
        cross = jnp.dot(high, small, preferred_element_type=jnp.float32)
        return both[:rows] + (both[rows:] + cross)

    def prepare(h):
        high, low = split(inverse[h])
        inv_high[h, :narrow, :narrow] = high
        inv_low[h, :narrow, :narrow] = low

    fetches[0].wait()
    prepare(half)

    @pl.when(half == 0)
    def _():
        loads[0].wait()

    fetches[1].wait()
    prepare(1 - half)
    slip_swap.wait_recv()
    force = apply(slip[...], half) + apply(other_slip[...], 1 - half)
    forces[body] = force.astype(jnp.bfloat16)
    held[...] = force

    def send(j):
        return pltpu.make_async_remote_copy(
            src_ref=forces.at[body],
            dst_ref=forces.at[body],
            send_sem=send_sems.at[j],
            recv_sem=recv_sems.at[body],
            device_id=cross(j),
            device_id_type=MESH,
        )

    slot = bodies - 1 - body
    doubled = (slot < extra) & jnp.logical_not(lead)

    def twin_send():
        return pltpu.make_async_remote_copy(
            src_ref=forces.at[body],
            dst_ref=twin_forces.at[slot],
            send_sem=twin_sems.at[extra],
            recv_sem=twin_sems.at[slot],
            device_id=same(0),
            device_id_type=MESH,
        )

    @pl.when(doubled)
    def _():
        twin_send().start()

    @pl.when(jnp.logical_not(lead))
    def _():
        send(0).start()

    if bodies > 2:

        @pl.when(jnp.logical_not(lead) & (half == 1))
        def _():
            pl.semaphore_wait(barrier, 2 * (bodies - 2))
            signal(go.at[1], {"col": partner})

        @pl.when(jnp.logical_not(lead) & (half == 0))
        def _():
            pl.semaphore_wait(go.at[1], 1)

    @pl.when(jnp.logical_not(lead))
    def _():
        others(lambda j: send(j).start())

    loads[1].wait()
    for a in range(3):
        source[a] = jnp.pad(positions[a], ((0, 0), (0, LANES - blobs)))
        for t in range(2):
            own_rows[3 * t + a : 3 * t + a + 1, :blobs] = positions[a, pl.ds(2 * body + t, 1), :]
    own_cols = own_rows[...].T
    for t in range(2):
        for a in range(3):
            own[t, a] = jnp.broadcast_to(
                own_cols[:pad, 3 * t + a : 3 * t + a + 1], (pad, LANES)
            )

    def send_on(j):
        pl.semaphore_wait(ready.at[j], 1)
        send(j).start()

    total_slots = jnp.where(lead, bodies + extra, bodies)
    early = jnp.where(lead, bodies // 2 - 1, 0)
    mid = jnp.where(lead, bodies // 2 + 1, 0)
    lax.fori_loop(0, mid, build, 0)
    loop(1, early + 1, send_on)
    lax.fori_loop(mid, total_slots, build, 0)

    @pl.when(lead)
    def _():
        loop(bodies // 2, bodies, send_on)


    def product(values, j):
        return lax.dot_general(
            values,
            tiles[j].reshape(6 * pad, wide),
            (((1,), (1,)), ((), ())),
            preferred_element_type=jnp.float32,
        )

    def receive(j):
        pltpu.make_async_remote_copy(
            src_ref=forces.at[j],
            dst_ref=forces.at[j],
            send_sem=send_sems.at[0],
            recv_sem=recv_sems.at[j],
            device_id={"col": partner},
            device_id_type=MESH,
        ).wait_recv()

    def twin_receive(f):
        pltpu.make_async_remote_copy(
            src_ref=twin_forces.at[f],
            dst_ref=twin_forces.at[f],
            send_sem=twin_sems.at[extra],
            recv_sem=twin_sems.at[f],
            device_id={"col": partner},
            device_id_type=MESH,
        ).wait_recv()

    def gather(picks):
        for j in picks:

            @pl.when(j != body)
            def _(j=j):
                receive(j)

        total = product(forces[picks[0]], picks[0])
        for j in picks[1:]:
            total = total + product(forces[j], j)
        return total

    def gather_run(start, stop):
        if stop - start <= 8:
            size = (stop - start + 1) // 2
            total = gather([far(bodies - 1 - k) for k in range(start, start + size)])
            return total + gather([far(bodies - 1 - k) for k in range(start + size, stop)])
        return lax.fori_loop(
            start,
            stop,
            lambda k, total: total + gather([far(bodies - 1 - k)]),
            jnp.zeros((slip.shape[0], 6 * pad), jnp.float32),
        )

    def compact(total):
        full = round_up(6 * pad, LANES)
        total = jnp.pad(total, ((0, 0), (0, full - 6 * pad)))
        lane = lax.broadcasted_iota(jnp.int32, total.shape, 1)

        def moved(by):
            return pltpu.roll(total, full - by, 1) if by else total

        values = []
        for t in range(2):
            start = 3 * t * pad
            shift = pad - blobs
            value = jnp.where(
                lane < blobs,
                moved(start),
                jnp.where(lane < 2 * blobs, moved(start + shift), moved(start + 2 * shift)),
            )
            values.append(value[:, :wide])
        return values

    def sent(j):
        send(j).wait_send()

    def all_sent():
        loop(0, body, sent)
        loop(body + 1, bodies, sent)

        @pl.when(doubled)
        def _():
            twin_send().wait_send()

        slip_swap.wait_send()

    part_swap = swap(part, other_part, part_sems)

    def share(total):
        for t, value in enumerate(compact(total)):
            part[t] = value
        part_swap.start()

    def settle(more):
        all_sent()
        part_swap.wait()
        sums = [part[t] + other_part[t] for t in (half, 1 - half)]
        if more:
            sums = [value + far_part[t] for value, t in zip(sums, (half, 1 - half))]
        mine = slip[...] - sums[0][:, :narrow]
        theirs = other_slip[...] - sums[1][:, :narrow]
        return mine, held[...] + (apply(mine, half) + apply(theirs, 1 - half))

    @pl.when(jnp.logical_not(lead))
    def _():
        share(gather_run(0, bodies))
        mine, result = settle(False)
        residual[0] = mine
        updated[0] = result[:, :narrow]

    @pl.when(lead)
    def _():
        row_at = lax.broadcasted_iota(jnp.int32, (wide, 3 * pad), 0)
        col_at = lax.broadcasted_iota(jnp.int32, (wide, 3 * pad), 1)
        gap = pad - blobs
        wanted = row_at + jnp.where(row_at < blobs, 0, jnp.where(row_at < 2 * blobs, gap, 2 * gap))
        picked = jnp.where((col_at == wanted) & (row_at < narrow), 1.0, 0.0).astype(jnp.bfloat16)
        for s, block in enumerate((bodies - 1, bodies)):
            rows = slice(s * wide, (s + 1) * wide)
            folded = jnp.zeros((wide, wide), jnp.float32)
            for t in range(2):
                tight = lax.dot_general(
                    tiles[block, t],
                    picked,
                    (((0,), (1,)), ((), ())),
                    preferred_element_type=jnp.float32,
                ).astype(jnp.bfloat16)
                turned[t] = tight
                for side in (inv_high, inv_low):
                    folded = folded + jnp.dot(tight, side[t], preferred_element_type=jnp.float32)
            high, low = split(folded)
            last[rows, :wide] = turned[half]
            last[rows, wide : 2 * wide] = high
            last[rows, 2 * wide :] = low

        share(gather_run(0, bodies - extra))

        if extra > 1:
            for f in range(1, extra):
                receive(bodies - 1 - f)
                twin_receive(f)
            total = jnp.zeros((slip.shape[0], 6 * pad), jnp.float32)
            for f in range(1, extra):
                total = total + product(forces[bodies - 1 - f], bodies - 1 - f)
                total = total + product(twin_forces[f], bodies + f)
            for t, value in enumerate(compact(total)):
                far_part[t] = value

        mine, result = settle(extra > 1)
        base[...] = mine
        held[...] = result

        receive(bodies - 1)
        twin_receive(0)
        final = jnp.dot(
            jnp.concatenate([forces[bodies - 1], twin_forces[0]], axis=1),
            last[...],
            preferred_element_type=jnp.float32,
        )
        residual[0] = base[...] - final[:, :narrow]
        change = final[:, wide : 2 * wide] + final[:, 2 * wide :]
        updated[0] = (held[...] - change)[:, :narrow]


def finish(updated, residual, updated_out, residual_out, sems):
    copies = [
        pltpu.make_async_copy(updated, updated_out, sems.at[0]),
        pltpu.make_async_copy(residual, residual_out, sems.at[1]),
    ]
    for copy in copies:
        copy.start()
    for copy in copies:
        copy.wait()


def stay(value):
    return pltpu.with_memory_space_constraint(value, pltpu.HBM)


def local(slip, inverse, positions):
    row_count = lax.axis_size("row")
    col_count = lax.axis_size("col")
    count = row_count * col_count
    bodies = count // 2
    blobs = positions.shape[2]
    rows, narrow = slip.shape[1:]
    wide = round_up(narrow, LANES)
    pad = round_up(blobs, CHUNK)
    vmem = pl.BlockSpec(memory_space=pltpu.VMEM)
    f32, bf16 = jnp.float32, jnp.bfloat16
    dma = pltpu.SemaphoreType.DMA
    extra = min(EXTRA, bodies // 2)
    tile_bytes = (bodies + extra) * 6 * pad * wide * 2
    updated, residual = pl.pallas_call(
        functools.partial(kernel, row_count, col_count, blobs, extra),
        out_shape=(
            pltpu.VMEM(slip.shape, f32),
            pltpu.VMEM(slip.shape, f32),
        ),
        in_specs=[pl.BlockSpec(memory_space=pltpu.HBM)] * 3,
        out_specs=(vmem, vmem),
        scratch_shapes=[
            pltpu.VMEM((rows, narrow), f32),
            pltpu.VMEM((2, narrow, narrow), f32),
            pltpu.VMEM((3, count, blobs), f32),
            pltpu.VMEM((2, wide, wide), bf16),
            pltpu.VMEM((2, wide, wide), bf16),
            pltpu.VMEM((bodies + extra, 2, 3 * pad, wide), bf16),
            pltpu.VMEM((8, LANES), f32),
            pltpu.VMEM((2, 3, pad, LANES), f32),
            pltpu.VMEM((3, count, LANES), f32),
            pltpu.VMEM((rows, narrow), f32),
            pltpu.VMEM((2, rows, wide), f32),
            pltpu.VMEM((2, rows, wide), f32),
            pltpu.VMEM((bodies, rows, wide), bf16),
            pltpu.VMEM((extra, rows, wide), bf16),
            pltpu.VMEM((rows, wide), f32),
            pltpu.VMEM((rows, narrow), f32),
            pltpu.VMEM((2, rows, wide), f32),
            pltpu.VMEM((2, wide, wide), bf16),
            pltpu.VMEM((2 * wide, 3 * wide), bf16),
            dma((4,)),
            dma((2,)),
            dma((2,)),
            dma((bodies,)),
            dma((bodies,)),
            dma((extra + 1,)),
            pltpu.SemaphoreType.REGULAR((2,)),
            pltpu.SemaphoreType.REGULAR((bodies,)),
        ],
        compiler_params=pltpu.CompilerParams(
            collective_id=0,
            has_side_effects=True,
            vmem_limit_bytes=min(tile_bytes + 16 * 2**20, 60 * 2**20),
        ),
    )(*(stay(v) for v in (slip, jnp.swapaxes(inverse, 0, 1), jnp.swapaxes(positions, 0, 1))))
    return pl.pallas_call(
        finish,
        out_shape=(jax.ShapeDtypeStruct(slip.shape, f32),) * 2,
        in_specs=[vmem, vmem],
        out_specs=(pl.BlockSpec(memory_space=pltpu.HBM),) * 2,
        scratch_shapes=[dma((2,))],
        compiler_params=pltpu.CompilerParams(vmem_limit_bytes=2**20),
    )(updated, residual)


def solution(mesh):
    in_specs = (
        P(("groups", "row", "col"), None, None),
        P(("groups", "row", "col"), None, None),
        P("groups", None, None),
    )
    out_specs = (P(("groups", "row", "col"), None, None), P(("groups", "row", "col"), None, None))
    return jax.shard_map(local, mesh=mesh, in_specs=in_specs, out_specs=out_specs, check_vma=False)
```

```python
import functools

import jax
import jax.numpy as jnp
from jax import lax
from jax.experimental import pallas as pl
from jax.experimental.pallas import tpu as pltpu
from jax.sharding import PartitionSpec as P

MESH = pl.DeviceIdType.MESH
LANES = 128
CHUNK = 16
EXTRA = 3


def round_up(value, step):
    return -(-value // step) * step


def split(value):
    high = value.astype(jnp.bfloat16)
    low = (value - high.astype(jnp.float32)).astype(jnp.bfloat16)
    return high, low


def kernel(
    row_count, col_count, blobs, extra,
    slip_hbm, inverse_hbm, positions_hbm,
    updated, residual,
    slip, inverse, positions,
    inv_high, inv_low, tiles, own_rows, own, source, other_slip, part, other_part,
    forces, twin_forces, held, base, far_part, turned, last,
    load_sems, swap_sems, send_sems, recv_sems, go, ready,
):
    bodies = row_count * col_count // 2
    row = lax.axis_index("row")
    col = lax.axis_index("col")
    half = lax.rem(col, 2)
    partner = col + 1 - 2 * half
    body = (row * col_count + col) // 2
    narrow = 3 * blobs
    wide = inv_high.shape[-1]
    pad = own.shape[2]
    middle = bodies // 2
    low_side = body < middle
    lead = body == 0

    def far(step):
        return jnp.where(low_side, bodies - 1 - step, step)

    def same(j):
        there = 2 * j + half
        return {"row": there // col_count, "col": lax.rem(there, col_count)}

    def cross(j):
        there = 2 * j + 1 - half
        return {"row": there // col_count, "col": lax.rem(there, col_count)}

    def loop(start, stop, action):
        def visit(j, carry):
            action(j)
            return carry

        lax.fori_loop(start, stop, visit, 0)

    def signal(sem, device):
        pl.semaphore_signal(sem, inc=1, device_id=device, device_id_type=MESH)

    barrier = pltpu.get_barrier_semaphore()

    def greet(j):
        there = 2 * j + jnp.where(lead, 0, 1)
        signal(barrier, {"row": there // col_count, "col": lax.rem(there, col_count)})

    def others(action):
        loop(1, body, action)
        loop(body + 1, bodies, action)

    @pl.when(lead)
    def _():
        loop(1, bodies, greet)

    def swap(source_ref, target_ref, which):
        return pltpu.make_async_remote_copy(
            src_ref=source_ref,
            dst_ref=target_ref,
            send_sem=swap_sems.at[0],
            recv_sem=swap_sems.at[which],
            device_id={"col": partner},
            device_id_type=MESH,
        )

    slip_swap = swap(slip_hbm.at[0], other_slip, 1)

    @pl.when(half == 1)
    def _():
        signal(barrier, {"col": partner})

    @pl.when(half == 0)
    def _():
        pl.semaphore_wait(barrier, jnp.where(lead, 1, 3))
        signal(go.at[0], {"col": partner})
        slip_swap.start()

    loads = [
        pltpu.make_async_copy(slip_hbm.at[0], slip, load_sems.at[0]),
        pltpu.make_async_copy(positions_hbm, positions, load_sems.at[1]),
    ]
    fetches = [
        pltpu.make_async_copy(
            inverse_hbm.at[pl.ds(h * narrow, narrow), 0, :], inverse.at[h], load_sems.at[2 + k]
        )
        for k, h in enumerate((half, 1 - half))
    ]
    for load in (loads[0], *fetches, loads[1]):
        load.start()

    @pl.when(jnp.logical_not(lead))
    def _():
        others(greet)

    @pl.when(half == 1)
    def _():
        loads[0].wait()
        pl.semaphore_wait(go.at[0], 1)
        swap(slip, other_slip, 1).start()

    @pl.when(jnp.logical_not(lead))
    def _():
        signal(ready.at[0], cross(0))

    inv_high[...] = jnp.zeros_like(inv_high)
    inv_low[...] = jnp.zeros_like(inv_low)
    own_rows[...] = jnp.zeros_like(own_rows)

    def build(step, carry):
        j = step
        here = jnp.where(j == body, half, 1 - half)
        block = jnp.where(j < bodies, 2 * j + here, 2 * (2 * bodies - 1 - j) + half)
        lane = lax.broadcasted_iota(jnp.int32, (CHUNK, LANES), 1)
        there = [
            jnp.broadcast_to(source[a, pl.ds(block, 1), :], (CHUNK, LANES)) for a in range(3)
        ]

        def spread(parts, group):
            value = None
            for b, part_b in enumerate(parts):
                start = b * blobs - group * LANES
                if start >= LANES or start + blobs <= 0:
                    continue
                value = part_b if value is None else jnp.where(lane < start, value, part_b)
            return value

        for t, at in [(t, at) for at in range(0, pad, CHUNK) for t in range(2)]:
            d = [own[t, a, at : at + CHUNK, :] - there[a] for a in range(3)]
            dist_sq = d[0] * d[0] + d[1] * d[1] + d[2] * d[2]
            r = lax.rsqrt(jnp.where(dist_sq > 0.0, dist_sq, 1.0))
            r2 = r * r
            k = 0.75 * r
            u = k * r2
            apart = dist_sq >= 4.0
            isotropic = jnp.where(
                apart, k + (2.0 / 3.0) * u, 1.0 - (9.0 / 32.0) * (dist_sq * r)
            )
            anisotropic = jnp.where(apart, u - (2.0 * u) * r2, (3.0 / 32.0) * r)
            scaled = [anisotropic * da for da in d]
            for a in range(3):
                parts = []
                for b in range(3):
                    value = scaled[min(a, b)] * d[max(a, b)]
                    if a == b:
                        value = value + isotropic
                    shift = b * blobs % LANES
                    parts.append(pltpu.roll(value, shift, 1) if shift else value)
                for group in range(wide // LANES):
                    tiles[
                        j,
                        t,
                        a * pad + at : a * pad + at + CHUNK,
                        group * LANES : (group + 1) * LANES,
                    ] = spread(parts, group).astype(jnp.bfloat16)
        return carry

    def apply(values, h):
        high, low = split(jnp.pad(values, ((0, 0), (0, wide - narrow))))
        big = inv_high[h]
        small = inv_low[h]
        rows = values.shape[0]
        both = jnp.dot(
            jnp.concatenate([high, low], axis=0), big, preferred_element_type=jnp.float32
        )
        cross = jnp.dot(high, small, preferred_element_type=jnp.float32)
        return both[:rows] + (both[rows:] + cross)

    def prepare(h):
        high, low = split(inverse[h])
        inv_high[h, :narrow, :narrow] = high
        inv_low[h, :narrow, :narrow] = low

    fetches[0].wait()
    prepare(half)

    @pl.when(half == 0)
    def _():
        loads[0].wait()

    fetches[1].wait()
    prepare(1 - half)
    slip_swap.wait_recv()
    force = apply(slip[...], half) + apply(other_slip[...], 1 - half)
    forces[body] = force.astype(jnp.bfloat16)
    held[...] = force

    slot = bodies - 1 - body

    def send(j):
        to_lead = jnp.where(slot == 0, 2, jnp.where(slot < extra, 1, 0))
        across = jnp.where(low_side == (j < middle), 0, 1)
        return pltpu.make_async_remote_copy(
            src_ref=forces.at[body],
            dst_ref=forces.at[body],
            send_sem=send_sems.at[0],
            recv_sem=recv_sems.at[jnp.where(j == 0, to_lead, across)],
            device_id=cross(j),
            device_id_type=MESH,
        )

    doubled = (slot < extra) & jnp.logical_not(lead)

    def twin_send():
        return pltpu.make_async_remote_copy(
            src_ref=forces.at[body],
            dst_ref=twin_forces.at[slot],
            send_sem=send_sems.at[0],
            recv_sem=recv_sems.at[jnp.where(slot == 0, 2, 1)],
            device_id=same(0),
            device_id_type=MESH,
        )

    @pl.when(doubled)
    def _():
        twin_send().start()

    @pl.when(jnp.logical_not(lead))
    def _():
        send(0).start()

    if bodies > 2:

        @pl.when(jnp.logical_not(lead) & (half == 1))
        def _():
            pl.semaphore_wait(barrier, 2 * (bodies - 2))
            signal(go.at[0], {"col": partner})

        @pl.when(jnp.logical_not(lead) & (half == 0))
        def _():
            pl.semaphore_wait(go.at[0], 1)

    @pl.when(jnp.logical_not(lead))
    def _():
        others(lambda j: send(j).start())

    loads[1].wait()
    for a in range(3):
        source[a] = jnp.pad(positions[a], ((0, 0), (0, LANES - blobs)))
        for t in range(2):
            own_rows[3 * t + a : 3 * t + a + 1, :blobs] = positions[a, pl.ds(2 * body + t, 1), :]
    own_cols = own_rows[...].T
    for t in range(2):
        for a in range(3):
            own[t, a] = jnp.broadcast_to(
                own_cols[:pad, 3 * t + a : 3 * t + a + 1], (pad, LANES)
            )

    total_slots = jnp.where(lead, bodies + extra, bodies)
    lax.fori_loop(0, total_slots, build, 0)

    @pl.when(lead)
    def _():
        pl.semaphore_wait(ready.at[0], bodies - 1)
        loop(1, bodies, lambda j: send(bodies - j).start())

    def product(values, j):
        return lax.dot_general(
            values,
            tiles[j].reshape(6 * pad, wide),
            (((1,), (1,)), ((), ())),
            preferred_element_type=jnp.float32,
        )

    def several(count):
        return pltpu.make_async_remote_copy(
            src_ref=forces.at[pl.ds(0, count)],
            dst_ref=forces.at[pl.ds(0, count)],
            send_sem=send_sems.at[0],
            recv_sem=recv_sems.at[0],
            device_id={"col": partner},
            device_id_type=MESH,
        )

    def receive(which, count):
        pltpu.make_async_remote_copy(
            src_ref=forces.at[pl.ds(0, count)],
            dst_ref=forces.at[pl.ds(0, count)],
            send_sem=send_sems.at[0],
            recv_sem=recv_sems.at[which],
            device_id={"col": partner},
            device_id_type=MESH,
        ).wait_recv()

    def gather(start, stop):
        picks = [far(bodies - 1 - k) for k in range(start, stop)] if stop - start <= 8 else None
        if picks:
            total = product(forces[picks[0]], picks[0])
            for j in picks[1:]:
                total = total + product(forces[j], j)
            return total

        def more(k, total):
            j = far(bodies - 1 - k)
            return total + product(forces[j], j)

        return lax.fori_loop(
            start, stop, more, jnp.zeros((slip.shape[0], 6 * pad), jnp.float32)
        )

    def compact(total):
        full = round_up(6 * pad, LANES)
        total = jnp.pad(total, ((0, 0), (0, full - 6 * pad)))
        lane = lax.broadcasted_iota(jnp.int32, total.shape, 1)

        def moved(by):
            return pltpu.roll(total, full - by, 1) if by else total

        values = []
        for t in range(2):
            start = 3 * t * pad
            shift = pad - blobs
            value = jnp.where(
                lane < blobs,
                moved(start),
                jnp.where(lane < 2 * blobs, moved(start + shift), moved(start + 2 * shift)),
            )
            values.append(value[:, :wide])
        return values

    def all_sent():
        @pl.when(doubled)
        def _():
            several(bodies).wait_send()

        @pl.when(jnp.logical_not(doubled))
        def _():
            several(bodies - 1).wait_send()

    part_swap = swap(part, other_part, 2)

    def share(total):
        for t, value in enumerate(compact(total)):
            part[t] = value
        slip_swap.wait_send()
        part_swap.start()

    def settle(more):
        all_sent()
        part_swap.wait()
        sums = [part[t] + other_part[t] for t in (half, 1 - half)]
        if more:
            sums = [value + far_part[t] for value, t in zip(sums, (half, 1 - half))]
        mine = slip[...] - sums[0][:, :narrow]
        theirs = other_slip[...] - sums[1][:, :narrow]
        return mine, held[...] + (apply(mine, half) + apply(theirs, 1 - half))

    @pl.when(jnp.logical_not(lead))
    def _():
        receive(0, middle - 1)
        total = gather(0, middle)
        receive(1, middle)
        share(total + gather(middle, bodies))
        mine, result = settle(False)
        residual[0] = mine
        updated[0] = result[:, :narrow]

    @pl.when(lead)
    def _():
        row_at = lax.broadcasted_iota(jnp.int32, (wide, 3 * pad), 0)
        col_at = lax.broadcasted_iota(jnp.int32, (wide, 3 * pad), 1)
        gap = pad - blobs
        wanted = row_at + jnp.where(row_at < blobs, 0, jnp.where(row_at < 2 * blobs, gap, 2 * gap))
        picked = jnp.where((col_at == wanted) & (row_at < narrow), 1.0, 0.0).astype(jnp.bfloat16)
        for s, block in enumerate((bodies - 1, bodies)):
            rows = slice(s * wide, (s + 1) * wide)
            folded = jnp.zeros((wide, wide), jnp.float32)
            for t in range(2):
                tight = lax.dot_general(
                    tiles[block, t],
                    picked,
                    (((0,), (1,)), ((), ())),
                    preferred_element_type=jnp.float32,
                ).astype(jnp.bfloat16)
                turned[t] = tight
                for side in (inv_high, inv_low):
                    folded = folded + jnp.dot(tight, side[t], preferred_element_type=jnp.float32)
            last[rows, :wide] = turned[half]
            last[rows, wide:] = folded.astype(jnp.bfloat16)

        receive(0, bodies - extra - 1)
        share(gather(0, bodies - extra))

        if extra > 1:
            receive(1, 2 * (extra - 1))
            total = jnp.zeros((slip.shape[0], 6 * pad), jnp.float32)
            for f in range(1, extra):
                total = total + product(forces[bodies - 1 - f], bodies - 1 - f)
                total = total + product(twin_forces[f], bodies + f)
            for t, value in enumerate(compact(total)):
                far_part[t] = value

        mine, result = settle(extra > 1)
        base[...] = mine
        held[...] = result

        receive(2, 2)
        final = jnp.dot(
            jnp.concatenate([forces[bodies - 1], twin_forces[0]], axis=1),
            last[...],
            preferred_element_type=jnp.float32,
        )
        residual[0] = base[...] - final[:, :narrow]
        updated[0] = (held[...] - final[:, wide:])[:, :narrow]


def finish(updated, residual, updated_out, residual_out, sems):
    copies = [
        pltpu.make_async_copy(updated, updated_out, sems.at[0]),
        pltpu.make_async_copy(residual, residual_out, sems.at[1]),
    ]
    for copy in copies:
        copy.start()
    for copy in copies:
        copy.wait()


def stay(value):
    return pltpu.with_memory_space_constraint(value, pltpu.HBM)


def local(slip, inverse, positions):
    row_count = lax.axis_size("row")
    col_count = lax.axis_size("col")
    count = row_count * col_count
    bodies = count // 2
    blobs = positions.shape[2]
    rows, narrow = slip.shape[1:]
    wide = round_up(narrow, LANES)
    pad = round_up(blobs, CHUNK)
    vmem = pl.BlockSpec(memory_space=pltpu.VMEM)
    f32, bf16 = jnp.float32, jnp.bfloat16
    dma = pltpu.SemaphoreType.DMA
    extra = min(EXTRA, bodies // 2)
    tile_bytes = (bodies + extra) * 6 * pad * wide * 2
    updated, residual = pl.pallas_call(
        functools.partial(kernel, row_count, col_count, blobs, extra),
        out_shape=(
            pltpu.VMEM(slip.shape, f32),
            pltpu.VMEM(slip.shape, f32),
        ),
        in_specs=[pl.BlockSpec(memory_space=pltpu.HBM)] * 3,
        out_specs=(vmem, vmem),
        scratch_shapes=[
            pltpu.VMEM((rows, narrow), f32),
            pltpu.VMEM((2, narrow, narrow), f32),
            pltpu.VMEM((3, count, blobs), f32),
            pltpu.VMEM((2, wide, wide), bf16),
            pltpu.VMEM((2, wide, wide), bf16),
            pltpu.VMEM((bodies + extra, 2, 3 * pad, wide), bf16),
            pltpu.VMEM((8, LANES), f32),
            pltpu.VMEM((2, 3, pad, LANES), f32),
            pltpu.VMEM((3, count, LANES), f32),
            pltpu.VMEM((rows, narrow), f32),
            pltpu.VMEM((2, rows, wide), f32),
            pltpu.VMEM((2, rows, wide), f32),
            pltpu.VMEM((bodies, rows, wide), bf16),
            pltpu.VMEM((extra, rows, wide), bf16),
            pltpu.VMEM((rows, wide), f32),
            pltpu.VMEM((rows, narrow), f32),
            pltpu.VMEM((2, rows, wide), f32),
            pltpu.VMEM((2, wide, wide), bf16),
            pltpu.VMEM((2 * wide, 2 * wide), bf16),
            dma((4,)),
            dma((3,)),
            dma((1,)),
            dma((3,)),
            pltpu.SemaphoreType.REGULAR((1,)),
            pltpu.SemaphoreType.REGULAR((1,)),
        ],
        compiler_params=pltpu.CompilerParams(
            collective_id=0,
            has_side_effects=True,
            vmem_limit_bytes=min(tile_bytes + 16 * 2**20, 60 * 2**20),
        ),
    )(*(stay(v) for v in (slip, jnp.swapaxes(inverse, 0, 1), jnp.swapaxes(positions, 0, 1))))
    return pl.pallas_call(
        finish,
        out_shape=(jax.ShapeDtypeStruct(slip.shape, f32),) * 2,
        in_specs=[vmem, vmem],
        out_specs=(pl.BlockSpec(memory_space=pltpu.HBM),) * 2,
        scratch_shapes=[dma((2,))],
        compiler_params=pltpu.CompilerParams(vmem_limit_bytes=2**20),
    )(updated, residual)


def solution(mesh):
    in_specs = (
        P(("groups", "row", "col"), None, None),
        P(("groups", "row", "col"), None, None),
        P("groups", None, None),
    )
    out_specs = (P(("groups", "row", "col"), None, None), P(("groups", "row", "col"), None, None))
    return jax.shard_map(local, mesh=mesh, in_specs=in_specs, out_specs=out_specs, check_vma=False)
```

```python
import functools

import jax
import jax.numpy as jnp
from jax import lax
from jax.experimental import pallas as pl
from jax.experimental.pallas import tpu as pltpu
from jax.sharding import PartitionSpec as P

MESH = pl.DeviceIdType.MESH
LANES = 128
CHUNK = 16
EXTRA = 3


def round_up(value, step):
    return -(-value // step) * step


def split(value):
    high = value.astype(jnp.bfloat16)
    low = (value - high.astype(jnp.float32)).astype(jnp.bfloat16)
    return high, low


def kernel(
    row_count, col_count, blobs, extra,
    slip_hbm, inverse_hbm, positions_hbm,
    updated, residual,
    slip, inverse, positions,
    inv_high, inv_low, tiles, own_rows, own, source, other_slip, part, other_part,
    forces, twin_forces, held, base, far_part, turned, last,
    load_sems, swap_sems, send_sems, recv_sems, go, ready,
):
    bodies = row_count * col_count // 2
    row = lax.axis_index("row")
    col = lax.axis_index("col")
    half = lax.rem(col, 2)
    partner = col + 1 - 2 * half
    body = (row * col_count + col) // 2
    narrow = 3 * blobs
    wide = inv_high.shape[-1]
    pad = own.shape[2]
    middle = bodies // 2
    low_side = body < middle
    lead = body == 0

    def far(step):
        return jnp.where(low_side, bodies - 1 - step, step)

    def same(j):
        there = 2 * j + half
        return {"row": there // col_count, "col": lax.rem(there, col_count)}

    def cross(j):
        there = 2 * j + 1 - half
        return {"row": there // col_count, "col": lax.rem(there, col_count)}

    def loop(start, stop, action):
        def visit(j, carry):
            action(j)
            return carry

        lax.fori_loop(start, stop, visit, 0)

    def signal(sem, device):
        pl.semaphore_signal(sem, inc=1, device_id=device, device_id_type=MESH)

    barrier = pltpu.get_barrier_semaphore()

    def greet(j):
        there = 2 * j + jnp.where(lead, 0, 1)
        signal(barrier, {"row": there // col_count, "col": lax.rem(there, col_count)})

    def others(action):
        loop(1, body, action)
        loop(body + 1, bodies, action)

    @pl.when(lead)
    def _():
        loop(1, bodies, greet)

    def swap(source_ref, target_ref, which):
        return pltpu.make_async_remote_copy(
            src_ref=source_ref,
            dst_ref=target_ref,
            send_sem=swap_sems.at[0],
            recv_sem=swap_sems.at[which],
            device_id={"col": partner},
            device_id_type=MESH,
        )

    slip_swap = swap(slip_hbm.at[0], other_slip, 1)

    @pl.when(half == 1)
    def _():
        signal(barrier, {"col": partner})

    @pl.when(half == 0)
    def _():
        pl.semaphore_wait(barrier, jnp.where(lead, 1, 3))
        signal(go.at[0], {"col": partner})
        slip_swap.start()

    loads = [
        pltpu.make_async_copy(slip_hbm.at[0], slip, load_sems.at[0]),
        pltpu.make_async_copy(positions_hbm, positions, load_sems.at[1]),
    ]
    fetches = [
        pltpu.make_async_copy(
            inverse_hbm.at[pl.ds(h * narrow, narrow), 0, :], inverse.at[h], load_sems.at[2 + k]
        )
        for k, h in enumerate((half, 1 - half))
    ]
    for load in (loads[0], *fetches, loads[1]):
        load.start()

    @pl.when(jnp.logical_not(lead))
    def _():
        others(greet)

    @pl.when(half == 1)
    def _():
        loads[0].wait()
        pl.semaphore_wait(go.at[0], 1)
        swap(slip, other_slip, 1).start()

    @pl.when(jnp.logical_not(lead))
    def _():
        signal(ready.at[jnp.where(low_side, 0, 1)], cross(0))

    inv_high[...] = jnp.zeros_like(inv_high)
    inv_low[...] = jnp.zeros_like(inv_low)
    own_rows[...] = jnp.zeros_like(own_rows)

    def build(step, carry):
        j = step
        here = jnp.where(j == body, half, 1 - half)
        block = jnp.where(j < bodies, 2 * j + here, 2 * (2 * bodies - 1 - j) + half)
        lane = lax.broadcasted_iota(jnp.int32, (CHUNK, LANES), 1)
        there = [
            jnp.broadcast_to(source[a, pl.ds(block, 1), :], (CHUNK, LANES)) for a in range(3)
        ]

        def spread(parts, group):
            value = None
            for b, part_b in enumerate(parts):
                start = b * blobs - group * LANES
                if start >= LANES or start + blobs <= 0:
                    continue
                value = part_b if value is None else jnp.where(lane < start, value, part_b)
            return value

        for t, at in [(t, at) for at in range(0, pad, CHUNK) for t in range(2)]:
            d = [own[t, a, at : at + CHUNK, :] - there[a] for a in range(3)]
            dist_sq = d[0] * d[0] + d[1] * d[1] + d[2] * d[2]
            r = lax.rsqrt(jnp.where(dist_sq > 0.0, dist_sq, 1.0))
            r2 = r * r
            k = 0.75 * r
            u = k * r2
            apart = dist_sq >= 4.0
            isotropic = jnp.where(
                apart, k + (2.0 / 3.0) * u, 1.0 - (9.0 / 32.0) * (dist_sq * r)
            )
            anisotropic = jnp.where(apart, u - (2.0 * u) * r2, (3.0 / 32.0) * r)
            scaled = [anisotropic * da for da in d]
            for a in range(3):
                parts = []
                for b in range(3):
                    value = scaled[min(a, b)] * d[max(a, b)]
                    if a == b:
                        value = value + isotropic
                    shift = b * blobs % LANES
                    parts.append(pltpu.roll(value, shift, 1) if shift else value)
                for group in range(wide // LANES):
                    tiles[
                        j,
                        t,
                        a * pad + at : a * pad + at + CHUNK,
                        group * LANES : (group + 1) * LANES,
                    ] = spread(parts, group).astype(jnp.bfloat16)
        return carry

    def apply(values, h):
        high, low = split(jnp.pad(values, ((0, 0), (0, wide - narrow))))
        big = inv_high[h]
        small = inv_low[h]
        rows = values.shape[0]
        both = jnp.dot(
            jnp.concatenate([high, low], axis=0), big, preferred_element_type=jnp.float32
        )
        cross = jnp.dot(high, small, preferred_element_type=jnp.float32)
        return both[:rows] + (both[rows:] + cross)

    def prepare(h):
        high, low = split(inverse[h])
        inv_high[h, :narrow, :narrow] = high
        inv_low[h, :narrow, :narrow] = low

    fetches[0].wait()
    prepare(half)

    @pl.when(half == 0)
    def _():
        loads[0].wait()

    force = apply(slip[...], half)
    fetches[1].wait()
    prepare(1 - half)
    slip_swap.wait_recv()
    force = force + apply(other_slip[...], 1 - half)
    forces[body] = force.astype(jnp.bfloat16)
    held[...] = force

    slot = bodies - 1 - body

    def send(j):
        to_lead = jnp.where(slot == 0, 2, jnp.where(slot < extra, 1, 0))
        across = jnp.where(low_side == (j < middle), 0, 1)
        return pltpu.make_async_remote_copy(
            src_ref=forces.at[body],
            dst_ref=forces.at[body],
            send_sem=send_sems.at[0],
            recv_sem=recv_sems.at[jnp.where(j == 0, to_lead, across)],
            device_id=cross(j),
            device_id_type=MESH,
        )

    doubled = (slot < extra) & jnp.logical_not(lead)

    def twin_send():
        return pltpu.make_async_remote_copy(
            src_ref=forces.at[body],
            dst_ref=twin_forces.at[slot],
            send_sem=send_sems.at[0],
            recv_sem=recv_sems.at[jnp.where(slot == 0, 2, 1)],
            device_id=same(0),
            device_id_type=MESH,
        )

    @pl.when(doubled)
    def _():
        twin_send().start()

    @pl.when(jnp.logical_not(lead))
    def _():
        send(0).start()

    if bodies > 2:

        @pl.when(jnp.logical_not(lead) & (half == 1))
        def _():
            pl.semaphore_wait(barrier, 2 * (bodies - 2))
            signal(go.at[0], {"col": partner})

        @pl.when(jnp.logical_not(lead) & (half == 0))
        def _():
            pl.semaphore_wait(go.at[0], 1)

    @pl.when(jnp.logical_not(lead))
    def _():
        others(lambda j: send(j).start())

    loads[1].wait()
    for a in range(3):
        source[a] = jnp.pad(positions[a], ((0, 0), (0, LANES - blobs)))
        for t in range(2):
            own_rows[3 * t + a : 3 * t + a + 1, :blobs] = positions[a, pl.ds(2 * body + t, 1), :]
    own_cols = own_rows[...].T
    for t in range(2):
        for a in range(3):
            own[t, a] = jnp.broadcast_to(
                own_cols[:pad, 3 * t + a : 3 * t + a + 1], (pad, LANES)
            )

    total_slots = jnp.where(lead, bodies + extra, bodies)
    early_slots = jnp.where(lead, middle + 1, 0)
    lax.fori_loop(0, early_slots, build, 0)

    @pl.when(lead)
    def _():
        pl.semaphore_wait(ready.at[0], middle - 1)
        loop(1, middle, lambda j: send(j).start())

    lax.fori_loop(early_slots, total_slots, build, 0)

    @pl.when(lead)
    def _():
        pl.semaphore_wait(ready.at[1], bodies - middle)
        loop(middle, bodies, lambda j: send(j).start())

    def product(values, j):
        return lax.dot_general(
            values,
            tiles[j].reshape(6 * pad, wide),
            (((1,), (1,)), ((), ())),
            preferred_element_type=jnp.float32,
        )

    def several(count):
        return pltpu.make_async_remote_copy(
            src_ref=forces.at[pl.ds(0, count)],
            dst_ref=forces.at[pl.ds(0, count)],
            send_sem=send_sems.at[0],
            recv_sem=recv_sems.at[0],
            device_id={"col": partner},
            device_id_type=MESH,
        )

    def receive(which, count):
        pltpu.make_async_remote_copy(
            src_ref=forces.at[pl.ds(0, count)],
            dst_ref=forces.at[pl.ds(0, count)],
            send_sem=send_sems.at[0],
            recv_sem=recv_sems.at[which],
            device_id={"col": partner},
            device_id_type=MESH,
        ).wait_recv()

    def gather(start, stop):
        picks = [far(bodies - 1 - k) for k in range(start, stop)] if stop - start <= 8 else None
        if picks:
            total = product(forces[picks[0]], picks[0])
            for j in picks[1:]:
                total = total + product(forces[j], j)
            return total

        def more(k, total):
            j = far(bodies - 1 - k)
            return total + product(forces[j], j)

        return lax.fori_loop(
            start, stop, more, jnp.zeros((slip.shape[0], 6 * pad), jnp.float32)
        )

    def compact(total):
        full = round_up(6 * pad, LANES)
        total = jnp.pad(total, ((0, 0), (0, full - 6 * pad)))
        lane = lax.broadcasted_iota(jnp.int32, total.shape, 1)

        def moved(by):
            return pltpu.roll(total, full - by, 1) if by else total

        values = []
        for t in range(2):
            start = 3 * t * pad
            shift = pad - blobs
            value = jnp.where(
                lane < blobs,
                moved(start),
                jnp.where(lane < 2 * blobs, moved(start + shift), moved(start + 2 * shift)),
            )
            values.append(value[:, :wide])
        return values

    def all_sent():
        @pl.when(doubled)
        def _():
            several(bodies).wait_send()

        @pl.when(jnp.logical_not(doubled))
        def _():
            several(bodies - 1).wait_send()

    part_swap = swap(part, other_part, 2)

    def share(total):
        for t, value in enumerate(compact(total)):
            part[t] = value
        slip_swap.wait_send()
        part_swap.start()

    def settle(more):
        all_sent()
        part_swap.wait()
        sums = [part[t] + other_part[t] for t in (half, 1 - half)]
        if more:
            sums = [value + far_part[t] for value, t in zip(sums, (half, 1 - half))]
        mine = slip[...] - sums[0][:, :narrow]
        theirs = other_slip[...] - sums[1][:, :narrow]
        return mine, held[...] + (apply(mine, half) + apply(theirs, 1 - half))

    @pl.when(jnp.logical_not(lead))
    def _():
        receive(0, middle - 1)
        total = gather(0, middle)
        receive(1, middle)
        share(total + gather(middle, bodies))
        mine, result = settle(False)
        residual[0] = mine
        updated[0] = result[:, :narrow]

    @pl.when(lead)
    def _():
        row_at = lax.broadcasted_iota(jnp.int32, (wide, 3 * pad), 0)
        col_at = lax.broadcasted_iota(jnp.int32, (wide, 3 * pad), 1)
        gap = pad - blobs
        wanted = row_at + jnp.where(row_at < blobs, 0, jnp.where(row_at < 2 * blobs, gap, 2 * gap))
        picked = jnp.where((col_at == wanted) & (row_at < narrow), 1.0, 0.0).astype(jnp.bfloat16)
        for s, block in enumerate((bodies - 1, bodies)):
            rows = slice(s * wide, (s + 1) * wide)
            folded = jnp.zeros((wide, wide), jnp.float32)
            for t in range(2):
                tight = lax.dot_general(
                    tiles[block, t],
                    picked,
                    (((0,), (1,)), ((), ())),
                    preferred_element_type=jnp.float32,
                ).astype(jnp.bfloat16)
                turned[t] = tight
                for side in (inv_high, inv_low):
                    folded = folded + jnp.dot(tight, side[t], preferred_element_type=jnp.float32)
            last[rows, :wide] = turned[half]
            last[rows, wide:] = folded.astype(jnp.bfloat16)

        receive(0, bodies - extra - 1)
        share(gather(0, bodies - extra))

        if extra > 1:
            receive(1, 2 * (extra - 1))
            total = jnp.zeros((slip.shape[0], 6 * pad), jnp.float32)
            for f in range(1, extra):
                total = total + product(forces[bodies - 1 - f], bodies - 1 - f)
                total = total + product(twin_forces[f], bodies + f)
            for t, value in enumerate(compact(total)):
                far_part[t] = value

        mine, result = settle(extra > 1)
        base[...] = mine
        held[...] = result

        receive(2, 2)
        final = jnp.dot(
            jnp.concatenate([forces[bodies - 1], twin_forces[0]], axis=1),
            last[...],
            preferred_element_type=jnp.float32,
        )
        residual[0] = base[...] - final[:, :narrow]
        updated[0] = (held[...] - final[:, wide:])[:, :narrow]


def finish(updated, residual, updated_out, residual_out, sems):
    copies = [
        pltpu.make_async_copy(updated, updated_out, sems.at[0]),
        pltpu.make_async_copy(residual, residual_out, sems.at[1]),
    ]
    for copy in copies:
        copy.start()
    for copy in copies:
        copy.wait()


def stay(value):
    return pltpu.with_memory_space_constraint(value, pltpu.HBM)


def local(slip, inverse, positions):
    row_count = lax.axis_size("row")
    col_count = lax.axis_size("col")
    count = row_count * col_count
    bodies = count // 2
    blobs = positions.shape[2]
    rows, narrow = slip.shape[1:]
    wide = round_up(narrow, LANES)
    pad = round_up(blobs, CHUNK)
    vmem = pl.BlockSpec(memory_space=pltpu.VMEM)
    f32, bf16 = jnp.float32, jnp.bfloat16
    dma = pltpu.SemaphoreType.DMA
    extra = min(EXTRA, bodies // 2)
    tile_bytes = (bodies + extra) * 6 * pad * wide * 2
    updated, residual = pl.pallas_call(
        functools.partial(kernel, row_count, col_count, blobs, extra),
        out_shape=(
            pltpu.VMEM(slip.shape, f32),
            pltpu.VMEM(slip.shape, f32),
        ),
        in_specs=[pl.BlockSpec(memory_space=pltpu.HBM)] * 3,
        out_specs=(vmem, vmem),
        scratch_shapes=[
            pltpu.VMEM((rows, narrow), f32),
            pltpu.VMEM((2, narrow, narrow), f32),
            pltpu.VMEM((3, count, blobs), f32),
            pltpu.VMEM((2, wide, wide), bf16),
            pltpu.VMEM((2, wide, wide), bf16),
            pltpu.VMEM((bodies + extra, 2, 3 * pad, wide), bf16),
            pltpu.VMEM((8, LANES), f32),
            pltpu.VMEM((2, 3, pad, LANES), f32),
            pltpu.VMEM((3, count, LANES), f32),
            pltpu.VMEM((rows, narrow), f32),
            pltpu.VMEM((2, rows, wide), f32),
            pltpu.VMEM((2, rows, wide), f32),
            pltpu.VMEM((bodies, rows, wide), bf16),
            pltpu.VMEM((extra, rows, wide), bf16),
            pltpu.VMEM((rows, wide), f32),
            pltpu.VMEM((rows, narrow), f32),
            pltpu.VMEM((2, rows, wide), f32),
            pltpu.VMEM((2, wide, wide), bf16),
            pltpu.VMEM((2 * wide, 2 * wide), bf16),
            dma((4,)),
            dma((3,)),
            dma((1,)),
            dma((3,)),
            pltpu.SemaphoreType.REGULAR((1,)),
            pltpu.SemaphoreType.REGULAR((2,)),
        ],
        compiler_params=pltpu.CompilerParams(
            collective_id=0,
            has_side_effects=True,
            vmem_limit_bytes=min(tile_bytes + 16 * 2**20, 60 * 2**20),
        ),
    )(*(stay(v) for v in (slip, jnp.swapaxes(inverse, 0, 1), jnp.swapaxes(positions, 0, 1))))
    return pl.pallas_call(
        finish,
        out_shape=(jax.ShapeDtypeStruct(slip.shape, f32),) * 2,
        in_specs=[vmem, vmem],
        out_specs=(pl.BlockSpec(memory_space=pltpu.HBM),) * 2,
        scratch_shapes=[dma((2,))],
        compiler_params=pltpu.CompilerParams(vmem_limit_bytes=2**20),
    )(updated, residual)


def solution(mesh):
    in_specs = (
        P(("groups", "row", "col"), None, None),
        P(("groups", "row", "col"), None, None),
        P("groups", None, None),
    )
    out_specs = (P(("groups", "row", "col"), None, None), P(("groups", "row", "col"), None, None))
    return jax.shard_map(local, mesh=mesh, in_specs=in_specs, out_specs=out_specs, check_vma=False)
```

```python
import functools

import jax
import jax.numpy as jnp
from jax import lax
from jax.experimental import pallas as pl
from jax.experimental.pallas import tpu as pltpu
from jax.sharding import PartitionSpec as P

MESH = pl.DeviceIdType.MESH
LANES = 128
CHUNK = 16
EXTRA = 4


def round_up(value, step):
    return -(-value // step) * step


def split(value):
    high = value.astype(jnp.bfloat16)
    low = (value - high.astype(jnp.float32)).astype(jnp.bfloat16)
    return high, low


def kernel(
    row_count, col_count, blobs, extra,
    slip_hbm, inverse_hbm, positions_hbm,
    updated, residual,
    slip, inverse, positions,
    inv_high, inv_low, tiles, own_rows, own, source, other_slip, part, other_part,
    forces, twin_forces, held, base, far_part, turned, last,
    load_sems, swap_sems, send_sems, recv_sems, go, ready,
):
    bodies = row_count * col_count // 2
    row = lax.axis_index("row")
    col = lax.axis_index("col")
    half = lax.rem(col, 2)
    partner = col + 1 - 2 * half
    body = (row * col_count + col) // 2
    narrow = 3 * blobs
    wide = inv_high.shape[-1]
    pad = own.shape[2]
    middle = bodies // 2
    low_side = body < middle
    lead = body == 0

    def far(step):
        return jnp.where(low_side, bodies - 1 - step, step)

    def same(j):
        there = 2 * j + half
        return {"row": there // col_count, "col": lax.rem(there, col_count)}

    def cross(j):
        there = 2 * j + 1 - half
        return {"row": there // col_count, "col": lax.rem(there, col_count)}

    def loop(start, stop, action):
        def visit(j, carry):
            action(j)
            return carry

        lax.fori_loop(start, stop, visit, 0)

    def signal(sem, device):
        pl.semaphore_signal(sem, inc=1, device_id=device, device_id_type=MESH)

    barrier = pltpu.get_barrier_semaphore()

    def greet(j):
        there = 2 * j + jnp.where(lead, 0, 1)
        signal(barrier, {"row": there // col_count, "col": lax.rem(there, col_count)})

    def others(action):
        loop(1, body, action)
        loop(body + 1, bodies, action)

    @pl.when(lead)
    def _():
        loop(1, bodies, greet)

    def swap(source_ref, target_ref, which):
        return pltpu.make_async_remote_copy(
            src_ref=source_ref,
            dst_ref=target_ref,
            send_sem=swap_sems.at[0],
            recv_sem=swap_sems.at[which],
            device_id={"col": partner},
            device_id_type=MESH,
        )

    slip_swap = swap(slip_hbm.at[0], other_slip, 1)

    @pl.when(half == 1)
    def _():
        signal(barrier, {"col": partner})

    @pl.when(half == 0)
    def _():
        pl.semaphore_wait(barrier, jnp.where(lead, 1, 3))
        signal(go.at[0], {"col": partner})
        slip_swap.start()

    loads = [
        pltpu.make_async_copy(slip_hbm.at[0], slip, load_sems.at[0]),
        pltpu.make_async_copy(positions_hbm, positions, load_sems.at[1]),
    ]
    fetches = [
        pltpu.make_async_copy(
            inverse_hbm.at[pl.ds(h * narrow, narrow), 0, :], inverse.at[h], load_sems.at[1 + k]
        )
        for k, h in enumerate((half, 1 - half))
    ]
    for load in (loads[0], *fetches):
        load.start()

    @pl.when(jnp.logical_not(lead))
    def _():
        others(greet)

    @pl.when(half == 1)
    def _():
        loads[0].wait()
        pl.semaphore_wait(go.at[0], 1)
        swap(slip, other_slip, 1).start()

    @pl.when(jnp.logical_not(lead))
    def _():
        signal(ready.at[jnp.where(low_side, 0, 1)], cross(0))

    inv_high[...] = jnp.zeros_like(inv_high)
    inv_low[...] = jnp.zeros_like(inv_low)
    own_rows[...] = jnp.zeros_like(own_rows)

    def build(step, carry):
        j = step
        here = jnp.where(j == body, half, 1 - half)
        block = jnp.where(j < bodies, 2 * j + here, 2 * (2 * bodies - 1 - j) + half)
        lane = lax.broadcasted_iota(jnp.int32, (CHUNK, LANES), 1)
        there = [
            jnp.broadcast_to(source[a, pl.ds(block, 1), :], (CHUNK, LANES)) for a in range(3)
        ]

        def spread(parts, group):
            value = None
            for b, part_b in enumerate(parts):
                start = b * blobs - group * LANES
                if start >= LANES or start + blobs <= 0:
                    continue
                value = part_b if value is None else jnp.where(lane < start, value, part_b)
            return value

        for t, at in [(t, at) for at in range(0, pad, CHUNK) for t in range(2)]:
            d = [own[t, a, at : at + CHUNK, :] - there[a] for a in range(3)]
            dist_sq = d[0] * d[0] + d[1] * d[1] + d[2] * d[2]
            r = lax.rsqrt(jnp.where(dist_sq > 0.0, dist_sq, 1.0))
            r2 = r * r
            k = 0.75 * r
            u = k * r2
            apart = dist_sq >= 4.0
            isotropic = jnp.where(
                apart, k + (2.0 / 3.0) * u, 1.0 - (9.0 / 32.0) * (dist_sq * r)
            )
            anisotropic = jnp.where(apart, u - (2.0 * u) * r2, (3.0 / 32.0) * r)
            scaled = [anisotropic * da for da in d]
            for a in range(3):
                parts = []
                for b in range(3):
                    value = scaled[min(a, b)] * d[max(a, b)]
                    if a == b:
                        value = value + isotropic
                    shift = b * blobs % LANES
                    parts.append(pltpu.roll(value, shift, 1) if shift else value)
                for group in range(wide // LANES):
                    tiles[
                        j,
                        t,
                        a * pad + at : a * pad + at + CHUNK,
                        group * LANES : (group + 1) * LANES,
                    ] = spread(parts, group).astype(jnp.bfloat16)
        return carry

    def apply(values, h):
        high, low = split(jnp.pad(values, ((0, 0), (0, wide - narrow))))
        big = inv_high[h]
        small = inv_low[h]
        rows = values.shape[0]
        both = jnp.dot(
            jnp.concatenate([high, low], axis=0), big, preferred_element_type=jnp.float32
        )
        cross = jnp.dot(high, small, preferred_element_type=jnp.float32)
        return both[:rows] + (both[rows:] + cross)

    def prepare(h):
        high, low = split(inverse[h])
        inv_high[h, :narrow, :narrow] = high
        inv_low[h, :narrow, :narrow] = low

    fetches[0].wait()
    loads[1].start()
    prepare(half)

    @pl.when(half == 0)
    def _():
        loads[0].wait()

    force = apply(slip[...], half)
    fetches[1].wait()
    prepare(1 - half)
    slip_swap.wait_recv()
    force = force + apply(other_slip[...], 1 - half)
    forces[body] = force.astype(jnp.bfloat16)
    held[...] = force

    slot = bodies - 1 - body

    def send(j):
        to_lead = jnp.where(slot == 0, 2, jnp.where(slot < extra, 1, 0))
        across = jnp.where(low_side == (j < middle), 0, 1)
        return pltpu.make_async_remote_copy(
            src_ref=forces.at[body],
            dst_ref=forces.at[body],
            send_sem=send_sems.at[0],
            recv_sem=recv_sems.at[jnp.where(j == 0, to_lead, across)],
            device_id=cross(j),
            device_id_type=MESH,
        )

    doubled = (slot < extra) & jnp.logical_not(lead)

    def twin_send():
        return pltpu.make_async_remote_copy(
            src_ref=forces.at[body],
            dst_ref=twin_forces.at[slot],
            send_sem=send_sems.at[0],
            recv_sem=recv_sems.at[jnp.where(slot == 0, 2, 1)],
            device_id=same(0),
            device_id_type=MESH,
        )

    @pl.when(doubled)
    def _():
        twin_send().start()

    @pl.when(jnp.logical_not(lead))
    def _():
        send(0).start()

    if bodies > 2:

        @pl.when(jnp.logical_not(lead) & (half == 1))
        def _():
            pl.semaphore_wait(barrier, 2 * (bodies - 2))
            signal(go.at[0], {"col": partner})

        @pl.when(jnp.logical_not(lead) & (half == 0))
        def _():
            pl.semaphore_wait(go.at[0], 1)

    @pl.when(jnp.logical_not(lead))
    def _():
        others(lambda j: send(j).start())

    loads[1].wait()
    for a in range(3):
        source[a] = jnp.pad(positions[a], ((0, 0), (0, LANES - blobs)))
        for t in range(2):
            own_rows[3 * t + a : 3 * t + a + 1, :blobs] = positions[a, pl.ds(2 * body + t, 1), :]
    own_cols = own_rows[...].T
    for t in range(2):
        for a in range(3):
            own[t, a] = jnp.broadcast_to(
                own_cols[:pad, 3 * t + a : 3 * t + a + 1], (pad, LANES)
            )

    total_slots = jnp.where(lead, bodies + extra, bodies)
    early_slots = jnp.where(lead, middle + 1, 0)
    lax.fori_loop(0, early_slots, build, 0)

    @pl.when(lead)
    def _():
        pl.semaphore_wait(ready.at[0], middle - 1)
        loop(1, middle, lambda j: send(j).start())

    lax.fori_loop(early_slots, total_slots, build, 0)

    @pl.when(lead)
    def _():
        pl.semaphore_wait(ready.at[1], bodies - middle)
        loop(middle, bodies, lambda j: send(j).start())

    def product(values, j):
        return lax.dot_general(
            values,
            tiles[j].reshape(6 * pad, wide),
            (((1,), (1,)), ((), ())),
            preferred_element_type=jnp.float32,
        )

    def several(count):
        return pltpu.make_async_remote_copy(
            src_ref=forces.at[pl.ds(0, count)],
            dst_ref=forces.at[pl.ds(0, count)],
            send_sem=send_sems.at[0],
            recv_sem=recv_sems.at[0],
            device_id={"col": partner},
            device_id_type=MESH,
        )

    def receive(which, count):
        pltpu.make_async_remote_copy(
            src_ref=forces.at[pl.ds(0, count)],
            dst_ref=forces.at[pl.ds(0, count)],
            send_sem=send_sems.at[0],
            recv_sem=recv_sems.at[which],
            device_id={"col": partner},
            device_id_type=MESH,
        ).wait_recv()

    def gather(start, stop):
        picks = [far(bodies - 1 - k) for k in range(start, stop)] if stop - start <= 8 else None
        if picks:
            total = product(forces[picks[0]], picks[0])
            for j in picks[1:]:
                total = total + product(forces[j], j)
            return total

        def more(k, total):
            j = far(bodies - 1 - k)
            return total + product(forces[j], j)

        return lax.fori_loop(
            start, stop, more, jnp.zeros((slip.shape[0], 6 * pad), jnp.float32)
        )

    def compact(total):
        full = round_up(6 * pad, LANES)
        total = jnp.pad(total, ((0, 0), (0, full - 6 * pad)))
        lane = lax.broadcasted_iota(jnp.int32, total.shape, 1)

        def moved(by):
            return pltpu.roll(total, full - by, 1) if by else total

        values = []
        for t in range(2):
            start = 3 * t * pad
            shift = pad - blobs
            value = jnp.where(
                lane < blobs,
                moved(start),
                jnp.where(lane < 2 * blobs, moved(start + shift), moved(start + 2 * shift)),
            )
            values.append(value[:, :wide])
        return values

    def all_sent():
        @pl.when(doubled)
        def _():
            several(bodies).wait_send()

        @pl.when(jnp.logical_not(doubled))
        def _():
            several(bodies - 1).wait_send()

    part_swap = swap(part, other_part, 2)

    def share(total):
        for t, value in enumerate(compact(total)):
            part[t] = value
        slip_swap.wait_send()
        part_swap.start()

    def settle(more):
        all_sent()
        part_swap.wait()
        sums = [part[t] + other_part[t] for t in (half, 1 - half)]
        if more:
            sums = [value + far_part[t] for value, t in zip(sums, (half, 1 - half))]
        mine = slip[...] - sums[0][:, :narrow]
        theirs = other_slip[...] - sums[1][:, :narrow]
        return mine, held[...] + (apply(mine, half) + apply(theirs, 1 - half))

    @pl.when(jnp.logical_not(lead))
    def _():
        receive(0, middle - 1)
        total = gather(0, middle)
        receive(1, middle)
        share(total + gather(middle, bodies))
        mine, result = settle(False)
        residual[0] = mine
        updated[0] = result[:, :narrow]

    @pl.when(lead)
    def _():
        row_at = lax.broadcasted_iota(jnp.int32, (wide, 3 * pad), 0)
        col_at = lax.broadcasted_iota(jnp.int32, (wide, 3 * pad), 1)
        gap = pad - blobs
        wanted = row_at + jnp.where(row_at < blobs, 0, jnp.where(row_at < 2 * blobs, gap, 2 * gap))
        picked = jnp.where((col_at == wanted) & (row_at < narrow), 1.0, 0.0).astype(jnp.bfloat16)
        for s, block in enumerate((bodies - 1, bodies)):
            rows = slice(s * wide, (s + 1) * wide)
            folded = jnp.zeros((wide, wide), jnp.float32)
            for t in range(2):
                tight = lax.dot_general(
                    tiles[block, t],
                    picked,
                    (((0,), (1,)), ((), ())),
                    preferred_element_type=jnp.float32,
                ).astype(jnp.bfloat16)
                turned[t] = tight
                for side in (inv_high, inv_low):
                    folded = folded + jnp.dot(tight, side[t], preferred_element_type=jnp.float32)
            last[rows, :wide] = turned[half]
            last[rows, wide:] = folded.astype(jnp.bfloat16)

        receive(0, bodies - extra - 1)
        share(gather(0, bodies - extra))

        if extra > 1:
            receive(1, 2 * (extra - 1))
            total = jnp.zeros((slip.shape[0], 6 * pad), jnp.float32)
            for f in range(1, extra):
                total = total + product(forces[bodies - 1 - f], bodies - 1 - f)
                total = total + product(twin_forces[f], bodies + f)
            for t, value in enumerate(compact(total)):
                far_part[t] = value

        mine, result = settle(extra > 1)
        base[...] = mine
        held[...] = result

        receive(2, 2)
        final = jnp.dot(
            jnp.concatenate([forces[bodies - 1], twin_forces[0]], axis=1),
            last[...],
            preferred_element_type=jnp.float32,
        )
        residual[0] = base[...] - final[:, :narrow]
        updated[0] = (held[...] - final[:, wide:])[:, :narrow]


def finish(updated, residual, updated_out, residual_out, sems):
    copies = [
        pltpu.make_async_copy(updated, updated_out, sems.at[0]),
        pltpu.make_async_copy(residual, residual_out, sems.at[1]),
    ]
    for copy in copies:
        copy.start()
    for copy in copies:
        copy.wait()


def stay(value):
    return pltpu.with_memory_space_constraint(value, pltpu.HBM)


def local(slip, inverse, positions):
    row_count = lax.axis_size("row")
    col_count = lax.axis_size("col")
    count = row_count * col_count
    bodies = count // 2
    blobs = positions.shape[2]
    rows, narrow = slip.shape[1:]
    wide = round_up(narrow, LANES)
    pad = round_up(blobs, CHUNK)
    vmem = pl.BlockSpec(memory_space=pltpu.VMEM)
    f32, bf16 = jnp.float32, jnp.bfloat16
    dma = pltpu.SemaphoreType.DMA
    extra = min(EXTRA, bodies // 2)
    tile_bytes = (bodies + extra) * 6 * pad * wide * 2
    updated, residual = pl.pallas_call(
        functools.partial(kernel, row_count, col_count, blobs, extra),
        out_shape=(
            pltpu.VMEM(slip.shape, f32),
            pltpu.VMEM(slip.shape, f32),
        ),
        in_specs=[pl.BlockSpec(memory_space=pltpu.HBM)] * 3,
        out_specs=(vmem, vmem),
        scratch_shapes=[
            pltpu.VMEM((rows, narrow), f32),
            pltpu.VMEM((2, narrow, narrow), f32),
            pltpu.VMEM((3, count, blobs), f32),
            pltpu.VMEM((2, wide, wide), bf16),
            pltpu.VMEM((2, wide, wide), bf16),
            pltpu.VMEM((bodies + extra, 2, 3 * pad, wide), bf16),
            pltpu.VMEM((8, LANES), f32),
            pltpu.VMEM((2, 3, pad, LANES), f32),
            pltpu.VMEM((3, count, LANES), f32),
            pltpu.VMEM((rows, narrow), f32),
            pltpu.VMEM((2, rows, wide), f32),
            pltpu.VMEM((2, rows, wide), f32),
            pltpu.VMEM((bodies, rows, wide), bf16),
            pltpu.VMEM((extra, rows, wide), bf16),
            pltpu.VMEM((rows, wide), f32),
            pltpu.VMEM((rows, narrow), f32),
            pltpu.VMEM((2, rows, wide), f32),
            pltpu.VMEM((2, wide, wide), bf16),
            pltpu.VMEM((2 * wide, 2 * wide), bf16),
            dma((3,)),
            dma((3,)),
            dma((1,)),
            dma((3,)),
            pltpu.SemaphoreType.REGULAR((1,)),
            pltpu.SemaphoreType.REGULAR((2,)),
        ],
        compiler_params=pltpu.CompilerParams(
            collective_id=0,
            has_side_effects=True,
            vmem_limit_bytes=min(tile_bytes + 16 * 2**20, 60 * 2**20),
        ),
    )(*(stay(v) for v in (slip, jnp.swapaxes(inverse, 0, 1), jnp.swapaxes(positions, 0, 1))))
    return pl.pallas_call(
        finish,
        out_shape=(jax.ShapeDtypeStruct(slip.shape, f32),) * 2,
        in_specs=[vmem, vmem],
        out_specs=(pl.BlockSpec(memory_space=pltpu.HBM),) * 2,
        scratch_shapes=[dma((2,))],
        compiler_params=pltpu.CompilerParams(vmem_limit_bytes=2**20),
    )(updated, residual)


def solution(mesh):
    in_specs = (
        P(("groups", "row", "col"), None, None),
        P(("groups", "row", "col"), None, None),
        P("groups", None, None),
    )
    out_specs = (P(("groups", "row", "col"), None, None), P(("groups", "row", "col"), None, None))
    return jax.shard_map(local, mesh=mesh, in_specs=in_specs, out_specs=out_specs, check_vma=False)
```

```python
import functools

import jax
import jax.numpy as jnp
from jax import lax
from jax.experimental import pallas as pl
from jax.experimental.pallas import tpu as pltpu
from jax.sharding import PartitionSpec as P

MESH = pl.DeviceIdType.MESH
LANES = 128
CHUNK = 16
EXTRA = 4


def round_up(value, step):
    return -(-value // step) * step


def split(value):
    high = value.astype(jnp.bfloat16)
    low = (value - high.astype(jnp.float32)).astype(jnp.bfloat16)
    return high, low


def kernel(
    row_count, col_count, blobs, extra,
    slip_hbm, inverse_hbm, positions_hbm,
    updated, residual,
    slip, inverse, positions,
    inv_high, inv_low, tiles, own_rows, own, source, other_slip, part, other_part,
    forces, twin_forces, held, base, far_part, turned, last,
    load_sems, swap_sems, send_sems, recv_sems, go, ready,
):
    bodies = row_count * col_count // 2
    row = lax.axis_index("row")
    col = lax.axis_index("col")
    half = lax.rem(col, 2)
    partner = col + 1 - 2 * half
    body = (row * col_count + col) // 2
    narrow = 3 * blobs
    wide = inv_high.shape[-1]
    pad = own.shape[2]
    middle = bodies // 2
    low_side = body < middle
    lead = body == 0

    def far(step):
        return jnp.where(low_side, bodies - 1 - step, step)

    def same(j):
        there = 2 * j + half
        return {"row": there // col_count, "col": lax.rem(there, col_count)}

    def cross(j):
        there = 2 * j + 1 - half
        return {"row": there // col_count, "col": lax.rem(there, col_count)}

    def loop(start, stop, action):
        def visit(j, carry):
            action(j)
            return carry

        lax.fori_loop(start, stop, visit, 0)

    def signal(sem, device):
        pl.semaphore_signal(sem, inc=1, device_id=device, device_id_type=MESH)

    barrier = pltpu.get_barrier_semaphore()

    def greet(j):
        there = 2 * j + jnp.where(lead, 0, 1)
        signal(barrier, {"row": there // col_count, "col": lax.rem(there, col_count)})

    def others(action):
        loop(1, body, action)
        loop(body + 1, bodies, action)

    @pl.when(lead)
    def _():
        loop(1, bodies, greet)

    def swap(source_ref, target_ref, which):
        return pltpu.make_async_remote_copy(
            src_ref=source_ref,
            dst_ref=target_ref,
            send_sem=swap_sems.at[0],
            recv_sem=swap_sems.at[which],
            device_id={"col": partner},
            device_id_type=MESH,
        )

    slip_swap = swap(slip_hbm.at[0], other_slip, 1)

    @pl.when(half == 1)
    def _():
        signal(barrier, {"col": partner})

    @pl.when(half == 0)
    def _():
        pl.semaphore_wait(barrier, jnp.where(lead, 1, 3))
        signal(go.at[0], {"col": partner})
        slip_swap.start()

    loads = [
        pltpu.make_async_copy(slip_hbm.at[0], slip, load_sems.at[0]),
        pltpu.make_async_copy(positions_hbm, positions, load_sems.at[1]),
    ]
    fetches = [
        pltpu.make_async_copy(
            inverse_hbm.at[pl.ds(h * narrow, narrow), 0, :], inverse.at[h], load_sems.at[1 + k]
        )
        for k, h in enumerate((half, 1 - half))
    ]
    for load in (loads[0], *fetches):
        load.start()

    @pl.when(jnp.logical_not(lead) & (half == 0))
    def _():
        others(greet)

    @pl.when(half == 1)
    def _():
        loads[0].wait()
        pl.semaphore_wait(go.at[0], 1)
        swap(slip, other_slip, 1).start()

    @pl.when(jnp.logical_not(lead))
    def _():
        signal(ready.at[jnp.where(low_side, 0, 1)], cross(0))

    inv_high[...] = jnp.zeros_like(inv_high)
    inv_low[...] = jnp.zeros_like(inv_low)
    own_rows[...] = jnp.zeros_like(own_rows)

    def build(step, carry):
        j = step
        here = jnp.where(j == body, half, 1 - half)
        block = jnp.where(j < bodies, 2 * j + here, 2 * (2 * bodies - 1 - j) + half)
        lane = lax.broadcasted_iota(jnp.int32, (CHUNK, LANES), 1)
        there = [
            jnp.broadcast_to(source[a, pl.ds(block, 1), :], (CHUNK, LANES)) for a in range(3)
        ]

        def spread(parts, group):
            value = None
            for b, part_b in enumerate(parts):
                start = b * blobs - group * LANES
                if start >= LANES or start + blobs <= 0:
                    continue
                value = part_b if value is None else jnp.where(lane < start, value, part_b)
            return value

        for t, at in [(t, at) for at in range(0, pad, CHUNK) for t in range(2)]:
            d = [own[t, a, at : at + CHUNK, :] - there[a] for a in range(3)]
            dist_sq = d[0] * d[0] + d[1] * d[1] + d[2] * d[2]
            r = lax.rsqrt(jnp.where(dist_sq > 0.0, dist_sq, 1.0))
            r2 = r * r
            k = 0.75 * r
            u = k * r2
            apart = dist_sq >= 4.0
            isotropic = jnp.where(
                apart, k + (2.0 / 3.0) * u, 1.0 - (9.0 / 32.0) * (dist_sq * r)
            )
            anisotropic = jnp.where(apart, u - (2.0 * u) * r2, (3.0 / 32.0) * r)
            scaled = [anisotropic * da for da in d]
            for a in range(3):
                parts = []
                for b in range(3):
                    value = scaled[min(a, b)] * d[max(a, b)]
                    if a == b:
                        value = value + isotropic
                    shift = b * blobs % LANES
                    parts.append(pltpu.roll(value, shift, 1) if shift else value)
                for group in range(wide // LANES):
                    tiles[
                        j,
                        t,
                        a * pad + at : a * pad + at + CHUNK,
                        group * LANES : (group + 1) * LANES,
                    ] = spread(parts, group).astype(jnp.bfloat16)
        return carry

    def apply(values, h):
        high, low = split(jnp.pad(values, ((0, 0), (0, wide - narrow))))
        big = inv_high[h]
        small = inv_low[h]
        rows = values.shape[0]
        both = jnp.dot(
            jnp.concatenate([high, low], axis=0), big, preferred_element_type=jnp.float32
        )
        cross = jnp.dot(high, small, preferred_element_type=jnp.float32)
        return both[:rows] + (both[rows:] + cross)

    def prepare(h):
        high, low = split(inverse[h])
        inv_high[h, :narrow, :narrow] = high
        inv_low[h, :narrow, :narrow] = low

    fetches[0].wait()
    loads[1].start()
    prepare(half)

    @pl.when(half == 0)
    def _():
        loads[0].wait()

    force = apply(slip[...], half)
    fetches[1].wait()
    prepare(1 - half)
    slip_swap.wait_recv()
    force = force + apply(other_slip[...], 1 - half)
    forces[body] = force.astype(jnp.bfloat16)
    held[...] = force

    slot = bodies - 1 - body

    def send(j):
        to_lead = jnp.where(slot == 0, 2, jnp.where(slot < extra, 1, 0))
        across = jnp.where(low_side == (j < middle), 0, 1)
        return pltpu.make_async_remote_copy(
            src_ref=forces.at[body],
            dst_ref=forces.at[body],
            send_sem=send_sems.at[0],
            recv_sem=recv_sems.at[jnp.where(j == 0, to_lead, across)],
            device_id=cross(j),
            device_id_type=MESH,
        )

    doubled = (slot < extra) & jnp.logical_not(lead)

    def twin_send():
        return pltpu.make_async_remote_copy(
            src_ref=forces.at[body],
            dst_ref=twin_forces.at[slot],
            send_sem=send_sems.at[0],
            recv_sem=recv_sems.at[jnp.where(slot == 0, 2, 1)],
            device_id=same(0),
            device_id_type=MESH,
        )

    @pl.when(doubled)
    def _():
        twin_send().start()

    @pl.when(jnp.logical_not(lead))
    def _():
        send(0).start()

    if bodies > 2:

        @pl.when(jnp.logical_not(lead) & (half == 1))
        def _():
            pl.semaphore_wait(barrier, bodies - 2)
            signal(go.at[0], {"col": partner})

        @pl.when(jnp.logical_not(lead) & (half == 0))
        def _():
            pl.semaphore_wait(go.at[0], 1)

    @pl.when(jnp.logical_not(lead))
    def _():
        others(lambda j: send(j).start())

    loads[1].wait()
    for a in range(3):
        source[a] = jnp.pad(positions[a], ((0, 0), (0, LANES - blobs)))
        for t in range(2):
            own_rows[3 * t + a : 3 * t + a + 1, :blobs] = positions[a, pl.ds(2 * body + t, 1), :]
    own_cols = own_rows[...].T
    for t in range(2):
        for a in range(3):
            own[t, a] = jnp.broadcast_to(
                own_cols[:pad, 3 * t + a : 3 * t + a + 1], (pad, LANES)
            )

    total_slots = jnp.where(lead, bodies + extra, bodies)
    early_slots = jnp.where(lead, middle + 1, 0)
    lax.fori_loop(0, early_slots, build, 0)

    @pl.when(lead)
    def _():
        pl.semaphore_wait(ready.at[0], middle - 1)
        loop(1, middle, lambda j: send(j).start())

    lax.fori_loop(early_slots, total_slots, build, 0)

    @pl.when(lead)
    def _():
        pl.semaphore_wait(ready.at[1], bodies - middle)
        loop(middle, bodies, lambda j: send(j).start())

    def product(values, j):
        return lax.dot_general(
            values,
            tiles[j].reshape(6 * pad, wide),
            (((1,), (1,)), ((), ())),
            preferred_element_type=jnp.float32,
        )

    def several(count):
        return pltpu.make_async_remote_copy(
            src_ref=forces.at[pl.ds(0, count)],
            dst_ref=forces.at[pl.ds(0, count)],
            send_sem=send_sems.at[0],
            recv_sem=recv_sems.at[0],
            device_id={"col": partner},
            device_id_type=MESH,
        )

    def receive(which, count):
        pltpu.make_async_remote_copy(
            src_ref=forces.at[pl.ds(0, count)],
            dst_ref=forces.at[pl.ds(0, count)],
            send_sem=send_sems.at[0],
            recv_sem=recv_sems.at[which],
            device_id={"col": partner},
            device_id_type=MESH,
        ).wait_recv()

    def gather(start, stop):
        picks = [far(bodies - 1 - k) for k in range(start, stop)] if stop - start <= 8 else None
        if picks:
            total = product(forces[picks[0]], picks[0])
            for j in picks[1:]:
                total = total + product(forces[j], j)
            return total

        def more(k, total):
            j = far(bodies - 1 - k)
            return total + product(forces[j], j)

        return lax.fori_loop(
            start, stop, more, jnp.zeros((slip.shape[0], 6 * pad), jnp.float32)
        )

    def compact(total):
        full = round_up(6 * pad, LANES)
        total = jnp.pad(total, ((0, 0), (0, full - 6 * pad)))
        lane = lax.broadcasted_iota(jnp.int32, total.shape, 1)

        def moved(by):
            return pltpu.roll(total, full - by, 1) if by else total

        values = []
        for t in range(2):
            start = 3 * t * pad
            shift = pad - blobs
            value = jnp.where(
                lane < blobs,
                moved(start),
                jnp.where(lane < 2 * blobs, moved(start + shift), moved(start + 2 * shift)),
            )
            values.append(value[:, :wide])
        return values

    def all_sent():
        @pl.when(doubled)
        def _():
            several(bodies).wait_send()

        @pl.when(jnp.logical_not(doubled))
        def _():
            several(bodies - 1).wait_send()

    part_swap = swap(part, other_part, 2)

    def share(total):
        for t, value in enumerate(compact(total)):
            part[t] = value
        slip_swap.wait_send()
        part_swap.start()

    def settle(more):
        all_sent()
        part_swap.wait()
        sums = [part[t] + other_part[t] for t in (half, 1 - half)]
        if more:
            sums = [value + far_part[t] for value, t in zip(sums, (half, 1 - half))]
        mine = slip[...] - sums[0][:, :narrow]
        theirs = other_slip[...] - sums[1][:, :narrow]
        return mine, held[...] + (apply(mine, half) + apply(theirs, 1 - half))

    @pl.when(jnp.logical_not(lead))
    def _():
        receive(0, middle - 1)
        total = gather(0, middle)
        receive(1, middle)
        share(total + gather(middle, bodies))
        mine, result = settle(False)
        residual[0] = mine
        updated[0] = result[:, :narrow]

    @pl.when(lead)
    def _():
        row_at = lax.broadcasted_iota(jnp.int32, (wide, 3 * pad), 0)
        col_at = lax.broadcasted_iota(jnp.int32, (wide, 3 * pad), 1)
        gap = pad - blobs
        wanted = row_at + jnp.where(row_at < blobs, 0, jnp.where(row_at < 2 * blobs, gap, 2 * gap))
        picked = jnp.where((col_at == wanted) & (row_at < narrow), 1.0, 0.0).astype(jnp.bfloat16)
        for s, block in enumerate((bodies - 1, bodies)):
            rows = slice(s * wide, (s + 1) * wide)
            folded = jnp.zeros((wide, wide), jnp.float32)
            for t in range(2):
                tight = lax.dot_general(
                    tiles[block, t],
                    picked,
                    (((0,), (1,)), ((), ())),
                    preferred_element_type=jnp.float32,
                ).astype(jnp.bfloat16)
                turned[t] = tight
                for side in (inv_high, inv_low):
                    folded = folded + jnp.dot(tight, side[t], preferred_element_type=jnp.float32)
            last[rows, :wide] = turned[half]
            last[rows, wide:] = folded.astype(jnp.bfloat16)

        receive(0, bodies - extra - 1)
        share(gather(0, bodies - extra))

        if extra > 1:
            receive(1, 2 * (extra - 1))
            total = jnp.zeros((slip.shape[0], 6 * pad), jnp.float32)
            for f in range(1, extra):
                total = total + product(forces[bodies - 1 - f], bodies - 1 - f)
                total = total + product(twin_forces[f], bodies + f)
            for t, value in enumerate(compact(total)):
                far_part[t] = value

        mine, result = settle(extra > 1)
        base[...] = mine
        held[...] = result

        receive(2, 2)
        final = jnp.dot(
            jnp.concatenate([forces[bodies - 1], twin_forces[0]], axis=1),
            last[...],
            preferred_element_type=jnp.float32,
        )
        residual[0] = base[...] - final[:, :narrow]
        updated[0] = (held[...] - final[:, wide:])[:, :narrow]


def finish(updated, residual, updated_out, residual_out, sems):
    copies = [
        pltpu.make_async_copy(updated, updated_out, sems.at[0]),
        pltpu.make_async_copy(residual, residual_out, sems.at[1]),
    ]
    for copy in copies:
        copy.start()
    for copy in copies:
        copy.wait()


def stay(value):
    return pltpu.with_memory_space_constraint(value, pltpu.HBM)


def local(slip, inverse, positions):
    row_count = lax.axis_size("row")
    col_count = lax.axis_size("col")
    count = row_count * col_count
    bodies = count // 2
    blobs = positions.shape[2]
    rows, narrow = slip.shape[1:]
    wide = round_up(narrow, LANES)
    pad = round_up(blobs, CHUNK)
    vmem = pl.BlockSpec(memory_space=pltpu.VMEM)
    f32, bf16 = jnp.float32, jnp.bfloat16
    dma = pltpu.SemaphoreType.DMA
    extra = min(EXTRA, bodies // 2)
    tile_bytes = (bodies + extra) * 6 * pad * wide * 2
    updated, residual = pl.pallas_call(
        functools.partial(kernel, row_count, col_count, blobs, extra),
        out_shape=(
            pltpu.VMEM(slip.shape, f32),
            pltpu.VMEM(slip.shape, f32),
        ),
        in_specs=[pl.BlockSpec(memory_space=pltpu.HBM)] * 3,
        out_specs=(vmem, vmem),
        scratch_shapes=[
            pltpu.VMEM((rows, narrow), f32),
            pltpu.VMEM((2, narrow, narrow), f32),
            pltpu.VMEM((3, count, blobs), f32),
            pltpu.VMEM((2, wide, wide), bf16),
            pltpu.VMEM((2, wide, wide), bf16),
            pltpu.VMEM((bodies + extra, 2, 3 * pad, wide), bf16),
            pltpu.VMEM((8, LANES), f32),
            pltpu.VMEM((2, 3, pad, LANES), f32),
            pltpu.VMEM((3, count, LANES), f32),
            pltpu.VMEM((rows, narrow), f32),
            pltpu.VMEM((2, rows, wide), f32),
            pltpu.VMEM((2, rows, wide), f32),
            pltpu.VMEM((bodies, rows, wide), bf16),
            pltpu.VMEM((extra, rows, wide), bf16),
            pltpu.VMEM((rows, wide), f32),
            pltpu.VMEM((rows, narrow), f32),
            pltpu.VMEM((2, rows, wide), f32),
            pltpu.VMEM((2, wide, wide), bf16),
            pltpu.VMEM((2 * wide, 2 * wide), bf16),
            dma((3,)),
            dma((3,)),
            dma((1,)),
            dma((3,)),
            pltpu.SemaphoreType.REGULAR((1,)),
            pltpu.SemaphoreType.REGULAR((2,)),
        ],
        compiler_params=pltpu.CompilerParams(
            collective_id=0,
            has_side_effects=True,
            vmem_limit_bytes=min(tile_bytes + 16 * 2**20, 60 * 2**20),
        ),
    )(*(stay(v) for v in (slip, jnp.swapaxes(inverse, 0, 1), jnp.swapaxes(positions, 0, 1))))
    return pl.pallas_call(
        finish,
        out_shape=(jax.ShapeDtypeStruct(slip.shape, f32),) * 2,
        in_specs=[vmem, vmem],
        out_specs=(pl.BlockSpec(memory_space=pltpu.HBM),) * 2,
        scratch_shapes=[dma((2,))],
        compiler_params=pltpu.CompilerParams(vmem_limit_bytes=2**20),
    )(updated, residual)


def solution(mesh):
    in_specs = (
        P(("groups", "row", "col"), None, None),
        P(("groups", "row", "col"), None, None),
        P("groups", None, None),
    )
    out_specs = (P(("groups", "row", "col"), None, None), P(("groups", "row", "col"), None, None))
    return jax.shard_map(local, mesh=mesh, in_specs=in_specs, out_specs=out_specs, check_vma=False)
```
